256 devices in a mesh: cluster: 64 (over x, z, y_lo), camera: 4 (over y_hi, core).
Axes of the slice: x: 4, y: 4 (y_hi: 2, y_lo: 2; y = y_hi * 2 + y_lo), z: 8, core: 2. Of those that a mesh axis runs over, the one named last changes fastest.
Arguments:
- counts: int32 [64], replicated, may hold values from 1 to 16, as said below
- tiles: int32 [1024, 4], replicated, may hold values from 0 to 3
- cam_jac: float32 [1024, 128, 512], P('cluster', None, 'camera'), may hold values from -0.6 to 0.6
- point_jac: float32 [1024, 128, 3, 512], P('cluster', None, None, 'camera'), may hold values from -0.15625 to 0.15625
- point_inv: float32 [1024, 3, 3, 512], P('cluster', None, None, 'camera'), may hold values from -1 to 1, as said below
Outputs:
- reduced: float32 [4, 512, 2048], P('camera', 'cluster')
The draws below stay inside these ranges and needn't reach their ends.
Inputs may be any that keep to these rules, and one draw needn't show every extreme that they name: For every device i below 32, exactly one of the devices i and i + 32 holds 13 to 16 live clusters and the other 1 to 8; at least 4 devices hold exactly 16. The live clusters of a device are its first counts slots. Every 3x3 block point_inv[c, :, :, p] is symmetric and positive definite.
All inputs are finite; a program needn't handle non-finite values.
Results may differ from the reference program's by a relative error of at most 0.0003.
Values sent between devices are 32-bit elements; how exact they have to be, the bound alone decides.
No kernel may reach another device: no remote copies, remote signals or barrier semaphores. Data moves between devices by JAX's collectives and lax.ppermute only.
A program may use at most 64 MiB of HBM per device.

```python
import jax
import jax.numpy as jnp
from jax import lax

CAMC = 512
PTS = 512
CAMS = 2048
ROWS = 128
KEEP = 12
EXTRA = 4
SLOTS = 16
CL_DEVICES = 64
CAM_DEVICES = 4
CLUSTERS = 1024
GT = 4


def draw_counts(key, part):
    half_count = CL_DEVICES // 2
    pair_order = jax.random.permutation(jax.random.fold_in(key, 11), half_count)
    pair_rank = jnp.argsort(pair_order, stable=True)
    upper_heavy = jax.random.randint(jax.random.fold_in(key, 12), (half_count,), 0, 2)
    surplus = jax.random.randint(jax.random.fold_in(key, 13), (half_count,), 1, EXTRA + 1)
    surplus = jnp.where(pair_rank < EXTRA, EXTRA, surplus)
    heavy_count = KEEP + surplus
    light_count = jax.random.randint(jax.random.fold_in(key, 14), (half_count,), 1, KEEP - EXTRA + 1)
    light_count = jnp.where(pair_rank == 0, 1, light_count)
    lower_half = jnp.where(upper_heavy == 0, heavy_count, light_count)
    upper_half = jnp.where(upper_heavy == 1, heavy_count, light_count)
    return jnp.concatenate([lower_half, upper_half]).astype(jnp.int32)


def draw_point_inv(key, part):
    shape = (CLUSTERS, 3, PTS)
    exponent = jax.random.uniform(jax.random.fold_in(key, 21), shape, jnp.float32, jnp.log(0.25), 0.0)
    diagonal_part = jnp.exp(exponent)
    magnitude = jax.random.uniform(jax.random.fold_in(key, 22), shape, jnp.float32, 0.2, 0.45)
    sign_flip = jnp.where(jax.random.bernoulli(jax.random.fold_in(key, 23), 0.5, shape), 1.0, -1.0)
    coupling_part = magnitude * sign_flip
    root_scale = jnp.sqrt(diagonal_part)
    pair_index = ((0, 0, 1), (0, 0, 2), (1, 2, 0))
    rows_list = []
    for first in range(3):
        entries = []
        for second in range(3):
            if first == second:
                entries.append(diagonal_part[:, first, :])
            else:
                which = pair_index[min(first, second)][max(first, second)]
                entries.append(root_scale[:, first, :] * root_scale[:, second, :] * coupling_part[:, which, :])
        rows_list.append(jnp.stack(entries, axis=1))
    return jnp.stack(rows_list, axis=1).astype(jnp.float32)


def touch_ends(values, key, smallest, top_value):
    spot = [jax.random.randint(jax.random.fold_in(key, axis), (), 0, length) for axis, length in enumerate(values.shape)]
    longest = values.shape.index(max(values.shape))
    neighbour = spot[:longest] + [(spot[longest] + 1) % values.shape[longest]] + spot[longest + 1:]
    return values.at[tuple(spot)].set(smallest).at[tuple(neighbour)].set(top_value)


def block_levels(stream_key, extent, pieces, smallest, top_value):
    def one(dim, shards_of):
        heights = jax.random.uniform(jax.random.fold_in(jax.random.fold_in(stream_key, 6), dim), (shards_of,), jnp.float32, smallest / len(pieces), top_value / len(pieces))
        return jnp.repeat(jnp.exp(heights), extent[dim] // shards_of).reshape((-1,) + (1,) * (len(extent) - dim - 1))

    factor_of = one(*pieces[0])
    for cut in pieces[1:]:
        factor_of = factor_of * one(*cut)
    return factor_of


def noise(stream_key, dims, deviation, most, split=(), kind=jnp.bfloat16):
    values = deviation * jax.random.normal(stream_key, dims, jnp.float32)
    if split:
        values = values * block_levels(stream_key, dims, split, -0.22, 0.18)
    return jnp.clip(values, -most, most).astype(kind)


def setup_inputs(seed: int = 0) -> dict:
    key_list = jax.random.split(jax.random.key(seed), 6)
    return {
        "counts": draw_counts(jax.random.fold_in(key_list[5], 71), 0),
        "tiles": touch_ends(jax.random.randint(key_list[1], (CLUSTERS, CAM_DEVICES), 0, GT), jax.random.fold_in(key_list[1], 1), 0, GT - 1).astype(jnp.int32),
        "cam_jac": noise(key_list[2], (CLUSTERS, ROWS, CAMC), 0.1, 0.6, ((0, 64), (2, 4)), jnp.float32),
        "point_jac": noise(key_list[3], (CLUSTERS, ROWS, 3, PTS), (3 * PTS) ** -0.5, 0.15625, ((0, 64), (3, 4)), jnp.float32),
        "point_inv": draw_point_inv(jax.random.fold_in(key_list[5], 71), 0),
    }


HIGHEST_PRECISION = lax.Precision.HIGHEST


def contract_rows(left, right):
    return lax.dot_general(left, right, (((0,), (0,)), ((), ())), precision=HIGHEST_PRECISION, preferred_element_type=jnp.float32)


def reference(counts, tiles, cam_jac, point_jac, point_inv):
    tile_width = CAMC // CAM_DEVICES
    within = jnp.arange(tile_width, dtype=jnp.int32)
    groups = jnp.arange(CAM_DEVICES, dtype=jnp.int32)

    def add_cluster(accumulator, cluster):
        panel = cam_jac[cluster]
        points = point_jac[cluster]
        inverse = point_inv[cluster]
        live = ((cluster % SLOTS) < counts[cluster // SLOTS]).astype(jnp.float32)
        weighted = jnp.einsum('rjp,jkp->rkp', points, inverse, precision=HIGHEST_PRECISION)
        coupled = jnp.dot(weighted.reshape(ROWS, -1), points.reshape(ROWS, -1).T, precision=HIGHEST_PRECISION, preferred_element_type=jnp.float32)
        schur = contract_rows(panel, panel - jnp.dot(coupled, panel, precision=HIGHEST_PRECISION, preferred_element_type=jnp.float32)) * live
        global_tiles = (groups * GT + tiles[cluster]).astype(jnp.int32)
        position = (global_tiles[:, None] * tile_width + within[None, :]).reshape(-1).astype(jnp.int32)
        accumulator = accumulator.at[position[:, None], position[None, :]].add(schur)
        return accumulator, None

    start = jnp.zeros((CAMS, CAMS), jnp.float32)
    total, _ = lax.scan(add_cluster, start, jnp.arange(CLUSTERS, dtype=jnp.int32))
    return total.reshape(CAM_DEVICES, CAMS // CAM_DEVICES, CAMS)
```

```python
import jax
import jax.numpy as jnp
from jax import lax
from jax.experimental import pallas as pl
from jax.experimental.pallas import tpu as pltpu
from jax.sharding import Mesh, PartitionSpec as P

W = 128
SLOTS = 16
HALF = SLOTS // 2
GT = 4
NX, NZ, NYL = 4, 8, 2
TILES = 3 * GT + 1
F32 = jnp.float32
BF16 = jnp.bfloat16


def split(value):
    high = value.astype(BF16)
    return high, (value - high.astype(F32)).astype(BF16)


def coupling_kernel(idx_ref, pts_ref, inv_ref, out_ref):
    slot = idx_ref[0] * HALF + pl.program_id(0)
    lane_row = lax.rem(slot, 8)
    pts = [pts_ref[0, j] for j in range(3)]
    pairs = []
    for k in range(3):
        weighted = None
        for j in range(3):
            scale = inv_ref[j, k, pl.ds(lane_row, 1), :]
            term = pts[j] * scale
            weighted = term if weighted is None else weighted + term
        pairs.append((split(weighted), split(pts[k])))
    left = jnp.concatenate([w[0] for w, _ in pairs] + [w[0] for w, _ in pairs] + [w[1] for w, _ in pairs], axis=1)
    right = jnp.concatenate([p[0] for _, p in pairs] + [p[1] for _, p in pairs] + [p[0] for _, p in pairs], axis=1)
    out_ref[0] = lax.dot_general(left, right, (((1,), (1,)), ((), ())), preferred_element_type=F32)


def coupling(which, pts, inv):
    return pl.pallas_call(
        coupling_kernel,
        out_shape=jax.ShapeDtypeStruct((HALF, W, W), F32),
        grid_spec=pltpu.PrefetchScalarGridSpec(
            num_scalar_prefetch=1,
            grid=(HALF,),
            in_specs=[
                pl.BlockSpec((1, 3, W, W), lambda i, idx: (idx[0] * HALF + i, 0, 0, 0)),
                pl.BlockSpec((3, 3, 8, W), lambda i, idx: (0, 0, idx[0], 0)),
            ],
            out_specs=pl.BlockSpec((1, W, W), lambda i, idx: (i, 0, 0)),
        ),
        cost_estimate=pl.CostEstimate(flops=HALF * 2 * 9 * W * W * W, bytes_accessed=HALF * 4 * W * W * 4, transcendentals=0),
        name="coupling",
    )(which, pts, inv)


def schur_kernel(meta_ref, tiles_ref, own_ref, oth_ref, c0_ref, c1_ref, c2_ref, c3_ref, acc_ref):
    phase = pl.program_id(0)
    step = pl.program_id(1)
    core = meta_ref[0]
    live = meta_ref[1]
    cam = meta_ref[2]
    half = lax.rem(core + phase, 2)
    slot = half * HALF + step

    @pl.when((phase == 0) & (step == 0))
    def _():
        acc_ref[...] = jnp.zeros_like(acc_ref)

    @pl.when(slot < live)
    def _():
        m_high, m_low = split(jnp.where(phase == 0, own_ref[0], oth_ref[0]))
        panel_t = c0_ref[0].T
        t_high, t_low = split(panel_t)
        prod = jnp.dot(
            jnp.concatenate([t_high, t_high, t_low], axis=1),
            jnp.concatenate([m_high, m_low, m_high], axis=0),
            preferred_element_type=F32,
        )
        r_high, r_low = split(panel_t - prod)
        left = jnp.concatenate([r_high, r_high, r_low], axis=1)
        parts = [split(ref[0]) for ref in (c0_ref, c1_ref, c2_ref, c3_ref)]
        right = jnp.concatenate(
            [
                jnp.concatenate([h for h, _ in parts], axis=1),
                jnp.concatenate([l for _, l in parts], axis=1),
                jnp.concatenate([h for h, _ in parts], axis=1),
            ],
            axis=0,
        )
        rows = jnp.dot(left, right, preferred_element_type=F32)
        row_tile = tiles_ref[slot * 4 + cam]
        for rel in range(4):
            block = rows[:, rel * W : (rel + 1) * W].reshape(NZ, NYL, 8, W)
            if rel == 0:
                tile = 3 * GT
            else:
                tile = (rel - 1) * GT + tiles_ref[slot * 4 + lax.bitwise_xor(cam, rel)]
            for yl in range(NYL):
                acc_ref[row_tile * NYL + yl, :, tile] += block[:, yl]


def schur(meta, tiles, own, oth, panels):
    def panel_map(p, j, meta_ref, tiles_ref):
        return (lax.rem(meta_ref[0] + p, 2) * HALF + j, 0, 0)

    panel = pl.BlockSpec((1, W, W), panel_map)
    shape = (NX * NYL, NZ, TILES, 8, W)
    return pl.pallas_call(
        schur_kernel,
        out_shape=jax.ShapeDtypeStruct(shape, F32),
        grid_spec=pltpu.PrefetchScalarGridSpec(
            num_scalar_prefetch=2,
            grid=(2, HALF),
            in_specs=[
                pl.BlockSpec((1, W, W), lambda p, j, m, t: (jnp.where(p == 0, j, HALF - 1), 0, 0)),
                pl.BlockSpec((1, W, W), lambda p, j, m, t: (jnp.where(p == 0, 0, j), 0, 0)),
                panel,
                panel,
                panel,
                panel,
            ],
            out_specs=pl.BlockSpec(shape, lambda p, j, m, t: (0, 0, 0, 0, 0)),
        ),
        cost_estimate=pl.CostEstimate(flops=SLOTS * 6 * 5 * W * W * W, bytes_accessed=SLOTS * 5 * W * W * 4, transcendentals=0),
        name="schur",
    )(meta, tiles, own, oth, *panels)


def place_kernel(meta_ref, in_ref, out_ref):
    cam = meta_ref[0]
    row_tile = meta_ref[1]
    out_ref[...] = jnp.zeros_like(out_ref)

    def total(tile):
        value = in_ref[0, tile]
        for z in range(1, NZ):
            value = value + in_ref[z, tile]
        return value

    for rel in range(1, 4):
        base = lax.bitwise_xor(cam, rel) * GT
        for t in range(GT):
            out_ref[0, :, pl.ds(pl.multiple_of((base + t) * W, W), W)] = total((rel - 1) * GT + t)
    out_ref[0, :, pl.ds(pl.multiple_of((cam * GT + row_tile) * W, W), W)] = total(3 * GT)


def place(meta, pieces):
    return pl.pallas_call(
        place_kernel,
        out_shape=jax.ShapeDtypeStruct((1, 8, 4 * GT * W), F32),
        grid_spec=pltpu.PrefetchScalarGridSpec(
            num_scalar_prefetch=1,
            grid=(1,),
            in_specs=[pl.BlockSpec((NZ, TILES, 8, W), lambda i, m: (0, 0, 0, 0))],
            out_specs=pl.BlockSpec((1, 8, 4 * GT * W), lambda i, m: (0, 0, 0)),
        ),
        name="place",
    )(meta, pieces)


def swap(value, axis):
    return lax.ppermute(value, axis, [(0, 1), (1, 0)])


def on_device(counts, tiles, cam_jac, point_jac, point_inv):
    x = lax.axis_index("x")
    z = lax.axis_index("z")
    yl = lax.axis_index("yl")
    yh = lax.axis_index("yh")
    core = lax.axis_index("c")
    device = (x * NZ + z) * NYL + yl
    cam = yh * 2 + core
    live = lax.dynamic_index_in_dim(counts, device, keepdims=False)
    local_tiles = lax.dynamic_slice_in_dim(tiles, device * SLOTS, SLOTS, 0).reshape(-1)

    pts = point_jac.transpose(0, 2, 1, 3)
    inv = point_inv.transpose(1, 2, 0, 3)

    c0 = cam_jac
    c2 = swap(c0, "yh")
    c1 = swap(c0, "c")

    m_send = coupling((1 - core)[None], pts, inv)
    m_recv = swap(m_send, "c")
    m_keep = coupling(core[None], pts, inv)
    m_chip = m_keep + m_recv
    m_own = m_chip + swap(m_chip, "yh")
    m_oth = swap(m_own, "c")
    c3 = swap(c2, "c")

    acc = schur(jnp.stack([core, live, cam]), local_tiles, m_own, m_oth, (c0, c1, c2, c3))
    got = lax.all_to_all(acc, ("x", "yl"), 0, 0, tiled=True)
    part = got.sum(axis=0)
    got = lax.all_to_all(part, "z", 0, 0, tiled=True)
    return place(jnp.stack([cam, x]), got)


def solution(mesh):
    fine = Mesh(mesh.devices.reshape(NX, NZ, NYL, 2, 2), ("x", "z", "yl", "yh", "c"))
    rows = ("x", "z", "yl")
    cams = ("yh", "c")
    in_specs = (
        P(),
        P(),
        P(rows, None, cams),
        P(rows, None, None, cams),
        P(rows, None, None, cams),
    )
    return jax.shard_map(
        on_device, mesh=fine, in_specs=in_specs, out_specs=P(cams, rows, None), check_vma=False
    )
```

```python
import jax
import jax.numpy as jnp
from jax import lax
from jax.experimental import pallas as pl
from jax.experimental.pallas import tpu as pltpu
from jax.sharding import Mesh, PartitionSpec as P

W = 128
SLOTS = 16
HALF = SLOTS // 2
CHUNK = 4
GT = 4
NX, NZH, NZL, NYL = 4, 4, 2, 2
FIRST = NX * NZL * NYL
TILES = 3 * GT + 1
F32 = jnp.float32
BF16 = jnp.bfloat16
ANY = pl.BlockSpec(memory_space=pl.ANY)
SMEM = pl.BlockSpec(memory_space=pltpu.SMEM)
VMEM = pl.BlockSpec(memory_space=pltpu.VMEM)


def split(value):
    high = value.astype(BF16)
    return high, (value - high.astype(F32)).astype(BF16)


def camera_index():
    return lax.axis_index("yh") * 2 + lax.axis_index("c")


def cluster_device():
    x, zh, zl, yl = (lax.axis_index(name) for name in ("x", "zh", "zl", "yl"))
    return ((x * NZH + zh) * NZL + zl) * NYL + yl


def coupling_kernel(mine, pts_hbm, inv_ref, out_ref, pts_buf, sems):
    core = lax.axis_index("c")
    base = (core if mine else 1 - core) * HALF

    def fetch(i):
        return pltpu.make_async_copy(pts_hbm.at[base + i], pts_buf.at[i], sems.at[i])

    for i in range(HALF):
        fetch(i).start()
    for i in range(HALF):
        fetch(i).wait()
        pts = [pts_buf[i, j] for j in range(3)]
        pairs = []
        for k in range(3):
            weighted = None
            for j in range(3):
                term = pts[j] * inv_ref[j, k, pl.ds(base + i, 1), :]
                weighted = term if weighted is None else weighted + term
            pairs.append((split(weighted), split(pts[k])))
        left = jnp.concatenate([w[0] for w, _ in pairs] + [w[0] for w, _ in pairs] + [w[1] for w, _ in pairs], axis=1)
        right = jnp.concatenate([p[0] for _, p in pairs] + [p[1] for _, p in pairs] + [p[0] for _, p in pairs], axis=1)
        out_ref[i] = lax.dot_general(left, right, (((1,), (1,)), ((), ())), preferred_element_type=F32)


def coupling(mine, pts, inv):
    def kernel(*refs):
        coupling_kernel(mine, *refs)

    return pl.pallas_call(
        kernel,
        out_shape=jax.ShapeDtypeStruct((HALF, W, W), F32),
        in_specs=[ANY, VMEM],
        out_specs=VMEM,
        scratch_shapes=[pltpu.VMEM((HALF, 3, W, W), F32), pltpu.SemaphoreType.DMA((HALF,))],
        cost_estimate=pl.CostEstimate(flops=HALF * 2 * 9 * W * W * W, bytes_accessed=HALF * 4 * W * W * 4, transcendentals=0),
        name="coupling",
    )(pts, inv)


def schur_kernel(counts_ref, tiles_ref, own_hbm, oth_hbm, c0_hbm, c1_hbm, c2_hbm, c3_hbm, acc_ref, m_buf, c_buf, m_sems, c_sems):
    core = lax.axis_index("c")
    cam = camera_index()
    device = cluster_device()
    live = counts_ref[device]
    panels = (c0_hbm, c1_hbm, c2_hbm, c3_hbm)

    def fetch_m(which):
        source, half = (own_hbm, core) if which == 0 else (oth_hbm, 1 - core)
        return pltpu.make_async_copy(source, m_buf.at[pl.ds(half * HALF, HALF)], m_sems.at[which])

    def fetch_c(rel, k):
        part = pl.ds(k * CHUNK, CHUNK)
        return pltpu.make_async_copy(panels[rel].at[part], c_buf.at[rel, part], c_sems.at[rel, k])

    steps = SLOTS // CHUNK
    for which in range(2):
        fetch_m(which).start()
    for k in range(steps):
        for rel in range(4):
            fetch_c(rel, k).start()
    acc_ref[...] = jnp.zeros_like(acc_ref)
    for which in range(2):
        fetch_m(which).wait()

    for k in range(steps):
        for rel in range(4):
            fetch_c(rel, k).wait()

        @pl.when(k * CHUNK < live)
        def _():
            for i in range(CHUNK):
                slot = k * CHUNK + i
                m_high, m_low = split(m_buf[slot])
                panel_t = c_buf[0, slot].T
                t_high, t_low = split(panel_t)
                prod = jnp.dot(
                    jnp.concatenate([t_high, t_high, t_low], axis=1),
                    jnp.concatenate([m_high, m_low, m_high], axis=0),
                    preferred_element_type=F32,
                )
                rest = panel_t - prod
                if i:
                    rest = jnp.where(slot < live, rest, 0.0)
                r_high, r_low = split(rest)
                left = jnp.concatenate([r_high, r_high, r_low], axis=1)
                parts = [split(c_buf[rel, slot]) for rel in range(4)]
                highs = jnp.concatenate([h for h, _ in parts], axis=1)
                lows = jnp.concatenate([l for _, l in parts], axis=1)
                right = jnp.concatenate([highs, lows, highs], axis=0)
                rows = jnp.dot(left, right, preferred_element_type=F32)
                row_tile = tiles_ref[cam, device * SLOTS + slot]
                for rel in range(4):
                    block = rows[:, rel * W : (rel + 1) * W].reshape(NZH, NZL, NYL, 8, W)
                    if rel == 0:
                        tile = 3 * GT
                    else:
                        tile = (rel - 1) * GT + tiles_ref[lax.bitwise_xor(cam, rel), device * SLOTS + slot]
                    for zl in range(NZL):
                        for yl in range(NYL):
                            acc_ref[row_tile * (NZL * NYL) + zl * NYL + yl, :, tile] += block[:, zl, yl]


def schur(counts, tiles, own, oth, panels):
    return pl.pallas_call(
        schur_kernel,
        out_shape=jax.ShapeDtypeStruct((FIRST, NZH, TILES, 8, W), F32),
        in_specs=[SMEM, SMEM] + [ANY] * 6,
        out_specs=VMEM,
        scratch_shapes=[
            pltpu.VMEM((SLOTS, W, W), F32),
            pltpu.VMEM((4, SLOTS, W, W), F32),
            pltpu.SemaphoreType.DMA((2,)),
            pltpu.SemaphoreType.DMA((4, SLOTS // CHUNK)),
        ],
        cost_estimate=pl.CostEstimate(flops=SLOTS * 6 * 5 * W * W * W, bytes_accessed=SLOTS * 5 * W * W * 4, transcendentals=0),
        name="schur",
    )(counts, tiles, own, oth, *panels)


def place_kernel(in_ref, out_ref):
    cam = camera_index()
    x = lax.axis_index("x")
    out_ref[...] = jnp.zeros_like(out_ref)

    def total(tile):
        value = in_ref[0, tile]
        for source in range(1, NZH):
            value = value + in_ref[source, tile]
        return value

    for rel in range(1, 4):
        base = lax.bitwise_xor(cam, rel) * GT
        for t in range(GT):
            out_ref[0, :, pl.ds(pl.multiple_of((base + t) * W, W), W)] = total((rel - 1) * GT + t)
    out_ref[0, :, pl.ds(pl.multiple_of((cam * GT + x) * W, W), W)] = total(3 * GT)


def place(pieces):
    return pl.pallas_call(
        place_kernel,
        out_shape=jax.ShapeDtypeStruct((1, 8, 4 * GT * W), F32),
        in_specs=[VMEM],
        out_specs=VMEM,
        name="place",
    )(pieces)


def swap(value, axis):
    return lax.ppermute(value, axis, [(0, 1), (1, 0)])


def on_device(counts, tiles, cam_jac, point_jac, point_inv):
    pts = point_jac.transpose(0, 2, 1, 3)
    inv = point_inv.transpose(1, 2, 0, 3)

    c0 = cam_jac
    c2 = swap(c0, "yh")
    c1 = swap(c0, "c")

    m_send = coupling(False, pts, inv)
    m_recv = swap(m_send, "c")
    m_keep = coupling(True, pts, inv)
    m_chip = m_keep + m_recv
    m_own = m_chip + swap(m_chip, "yh")
    m_oth = swap(m_own, "c")
    c3 = swap(c2, "c")

    acc = schur(counts, tiles.T, m_own, m_oth, (c0, c1, c2, c3))
    got = lax.all_to_all(acc, ("x", "zl", "yl"), 0, 0, tiled=True)
    part = got.sum(axis=0)
    return place(lax.all_to_all(part, "zh", 0, 0, tiled=True))


def solution(mesh):
    fine = Mesh(mesh.devices.reshape(NX, NZH, NZL, NYL, 2, 2), ("x", "zh", "zl", "yl", "yh", "c"))
    rows = ("x", "zh", "zl", "yl")
    cams = ("yh", "c")
    in_specs = (
        P(),
        P(),
        P(rows, None, cams),
        P(rows, None, None, cams),
        P(rows, None, None, cams),
    )
    return jax.shard_map(
        on_device, mesh=fine, in_specs=in_specs, out_specs=P(cams, rows, None), check_vma=False
    )
```

```python
import jax
import jax.numpy as jnp
from jax import lax
from jax.experimental import pallas as pl
from jax.experimental.pallas import tpu as pltpu
from jax.sharding import Mesh, PartitionSpec as P


W = 128
SLOTS = 16
HALF = SLOTS // 2
CHUNK = 4
GT = 4
NXH, NXL, NZH, NZL, NYL = 2, 2, 4, 2, 2
GROUPS = (("xl", "zl", "yl", GT), ("zl", "yl", "xl", GT), ("yl", "xl", "zl", GT + 1))
F32 = jnp.float32
BF16 = jnp.bfloat16
ANY = pl.BlockSpec(memory_space=pl.ANY)
SMEM = pl.BlockSpec(memory_space=pltpu.SMEM)
VMEM = pl.BlockSpec(memory_space=pltpu.VMEM)


def split(value):
    high = value.astype(BF16)
    return high, (value - high.astype(F32)).astype(BF16)


def camera_index():
    return lax.axis_index("yh") * 2 + lax.axis_index("c")


def cluster_device():
    xh, xl, zh, zl, yl = (lax.axis_index(name) for name in ("xh", "xl", "zh", "zl", "yl"))
    return (((xh * NXL + xl) * NZH + zh) * NZL + zl) * NYL + yl


def coupling_kernel(mine, pts_hbm, inv_ref, out_ref, pts_buf, sems):
    core = lax.axis_index("c")
    base = (core if mine else 1 - core) * HALF

    def fetch(i):
        return pltpu.make_async_copy(pts_hbm.at[base + i], pts_buf.at[i], sems.at[i])

    for i in range(HALF):
        fetch(i).start()
    for i in range(HALF):
        fetch(i).wait()
        pts = [pts_buf[i, j] for j in range(3)]
        pairs = []
        for k in range(3):
            weighted = None
            for j in range(3):
                term = pts[j] * inv_ref[j, k, pl.ds(base + i, 1), :]
                weighted = term if weighted is None else weighted + term
            pairs.append((split(weighted), split(pts[k])))
        left = jnp.concatenate([w[0] for w, _ in pairs] + [w[0] for w, _ in pairs] + [w[1] for w, _ in pairs], axis=1)
        right = jnp.concatenate([p[0] for _, p in pairs] + [p[1] for _, p in pairs] + [p[0] for _, p in pairs], axis=1)
        out_ref[i] = lax.dot_general(left, right, (((1,), (1,)), ((), ())), preferred_element_type=F32)


def coupling(mine, pts, inv):
    def kernel(*refs):
        coupling_kernel(mine, *refs)

    return pl.pallas_call(
        kernel,
        out_shape=jax.ShapeDtypeStruct((HALF, W, W), F32),
        in_specs=[ANY, VMEM],
        out_specs=VMEM,
        scratch_shapes=[pltpu.VMEM((HALF, 3, W, W), F32), pltpu.SemaphoreType.DMA((HALF,))],
        cost_estimate=pl.CostEstimate(flops=HALF * 2 * 9 * W * W * W, bytes_accessed=HALF * 4 * W * W * 4, transcendentals=0),
        name="coupling",
    )(pts, inv)


def schur_kernel(counts_ref, tiles_ref, own_hbm, oth_hbm, c0_hbm, c1_hbm, c2_hbm, c3_hbm, *refs):
    outs, (m_buf, c_buf, m_sems, c_sems, o_sems), accs = refs[:6], refs[6:11], refs[11:]
    core = lax.axis_index("c")
    cam = camera_index()
    device = cluster_device()
    live = counts_ref[device]
    panels = (c0_hbm, c1_hbm, c2_hbm, c3_hbm)

    def fetch_m(which):
        source, half = (own_hbm, core) if which == 0 else (oth_hbm, 1 - core)
        return pltpu.make_async_copy(source, m_buf.at[pl.ds(half * HALF, HALF)], m_sems.at[which])

    def fetch_c(rel, k):
        part = pl.ds(k * CHUNK, CHUNK)
        return pltpu.make_async_copy(panels[rel].at[part], c_buf.at[rel, part], c_sems.at[rel, k])

    steps = SLOTS // CHUNK
    for which in range(2):
        fetch_m(which).start()
    for k in range(steps):
        for rel in range(4):
            fetch_c(rel, k).start()
    for acc in accs:
        acc[...] = jnp.zeros_like(acc)
    for which in range(2):
        fetch_m(which).wait()

    for k in range(steps):
        for rel in range(4):
            fetch_c(rel, k).wait()

        @pl.when(k * CHUNK < live)
        def _():
            for i in range(CHUNK):
                slot = k * CHUNK + i
                m_high, m_low = split(m_buf[slot])
                panel_t = c_buf[0, slot].T
                t_high, t_low = split(panel_t)
                prod = jnp.dot(
                    jnp.concatenate([t_high, t_high, t_low], axis=1),
                    jnp.concatenate([m_high, m_low, m_high], axis=0),
                    preferred_element_type=F32,
                )
                rest = panel_t - prod
                if i:
                    rest = jnp.where(slot < live, rest, 0.0)
                r_high, r_low = split(rest)
                left = jnp.concatenate([r_high, r_high, r_low], axis=1)
                parts = [split(c_buf[rel, slot]) for rel in range(4)]
                highs = jnp.concatenate([h for h, _ in parts], axis=1)
                lows = jnp.concatenate([l for _, l in parts], axis=1)
                right = jnp.concatenate([highs, lows, highs], axis=0)
                rows = jnp.dot(left, right, preferred_element_type=F32)
                row_tile = tiles_ref[cam, device * SLOTS + slot]
                for rel in range(4):
                    block = rows[:, rel * W : (rel + 1) * W].reshape(NZH, NZL, NYL, 8, W)
                    if rel == 0:
                        group, tile = 2, GT
                    else:
                        group, tile = rel - 1, tiles_ref[lax.bitwise_xor(cam, rel), device * SLOTS + slot]
                    for zl in range(NZL):
                        for yl in range(NYL):
                            place_at = {"xl": lax.rem(row_tile, NXL), "zl": zl, "yl": yl}
                            lead = tuple(place_at[name] for name in GROUPS[group][:3])
                            accs[group][lead + (row_tile // NXL, slice(None), tile)] += block[:, zl, yl]

    copies = []
    for group, names in enumerate(GROUPS):
        bit = lax.axis_index(names[0])
        for which, source in enumerate((1 - bit, bit)):
            k = group * 2 + which
            copies.append(pltpu.make_async_copy(accs[group].at[source], outs[k], o_sems.at[k]))
    for copy in copies:
        copy.start()
    for copy in copies:
        copy.wait()


def schur(counts, tiles, own, oth, panels):
    return pl.pallas_call(
        schur_kernel,
        out_shape=[jax.ShapeDtypeStruct((2, 2, NXH, NZH, names[3], 8, W), F32) for names in GROUPS for _ in range(2)],
        in_specs=[SMEM, SMEM] + [ANY] * 6,
        out_specs=[ANY] * 6,
        scratch_shapes=[
            pltpu.VMEM((SLOTS, W, W), F32),
            pltpu.VMEM((4, SLOTS, W, W), F32),
            pltpu.SemaphoreType.DMA((2,)),
            pltpu.SemaphoreType.DMA((4, SLOTS // CHUNK)),
            pltpu.SemaphoreType.DMA((6,)),
        ]
        + [pltpu.VMEM((2, 2, 2, NXH, NZH, names[3], 8, W), F32) for names in GROUPS],
        cost_estimate=pl.CostEstimate(flops=SLOTS * 6 * 5 * W * W * W, bytes_accessed=SLOTS * 5 * W * W * 4, transcendentals=0),
        name="schur",
    )(counts, tiles, own, oth, *panels)


def place_kernel(in_ref, out_ref):
    cam = camera_index()
    x = lax.axis_index("xh") * NXL + lax.axis_index("xl")
    out_ref[...] = jnp.zeros_like(out_ref)

    def total(tile):
        value = in_ref[0, tile]
        for source in range(1, NXH * NZH):
            value = value + in_ref[source, tile]
        return value

    for rel in range(1, 4):
        base = lax.bitwise_xor(cam, rel) * GT
        for t in range(GT):
            out_ref[0, :, pl.ds(pl.multiple_of((base + t) * W, W), W)] = total((rel - 1) * GT + t)
    out_ref[0, :, pl.ds(pl.multiple_of((cam * GT + x) * W, W), W)] = total(3 * GT)


def place(pieces):
    return pl.pallas_call(
        place_kernel,
        out_shape=jax.ShapeDtypeStruct((1, 8, 4 * GT * W), F32),
        in_specs=[VMEM],
        out_specs=VMEM,
        name="place",
    )(pieces)


def swap(value, axis):
    return lax.ppermute(value, axis, [(0, 1), (1, 0)])


def on_device(counts, tiles, cam_jac, point_jac, point_inv):
    pts = point_jac.transpose(0, 2, 1, 3)
    inv = point_inv.transpose(1, 2, 0, 3)

    c0 = cam_jac
    c2 = swap(c0, "yh")
    c1 = swap(c0, "c")

    m_send = coupling(False, pts, inv)
    m_recv = swap(m_send, "c")
    m_keep = coupling(True, pts, inv)
    m_chip = m_keep + m_recv
    m_own = m_chip + swap(m_chip, "yh")
    m_oth = swap(m_own, "c")
    c3 = swap(c2, "c")

    outs = schur(counts, tiles.T, m_own, m_oth, (c0, c1, c2, c3))
    groups = [(outs[2 * k], outs[2 * k + 1]) for k in range(3)]
    for phase in range(3):
        received = []
        for k, (send, _) in enumerate(groups):
            received.append(swap(send, GROUPS[k][phase]))
        if phase == 2:
            break
        split_groups = []
        for k, (_, keep) in enumerate(groups):
            bit = lax.axis_index(GROUPS[k][phase + 1])
            halves = [
                lax.dynamic_index_in_dim(keep, at, keepdims=False)
                + lax.dynamic_index_in_dim(received[k], at, keepdims=False)
                for at in (1 - bit, bit)
            ]
            split_groups.append(tuple(halves))
        groups = split_groups
    part = jnp.concatenate(
        [(keep + got).reshape(NXH * NZH, -1, 8, W) for (_, keep), got in zip(groups, received)], axis=1
    )
    return place(lax.all_to_all(part, ("xh", "zh"), 0, 0, tiled=True))


def solution(mesh):
    fine = Mesh(mesh.devices.reshape(NXH, NXL, NZH, NZL, NYL, 2, 2), ("xh", "xl", "zh", "zl", "yl", "yh", "c"))
    rows = ("xh", "xl", "zh", "zl", "yl")
    cams = ("yh", "c")
    in_specs = (
        P(),
        P(),
        P(rows, None, cams),
        P(rows, None, None, cams),
        P(rows, None, None, cams),
    )
    return jax.shard_map(
        on_device, mesh=fine, in_specs=in_specs, out_specs=P(cams, rows, None), check_vma=False
    )
```

```python
import jax
import jax.numpy as jnp
from jax import lax
from jax.experimental import pallas as pl
from jax.experimental.pallas import tpu as pltpu
from jax.sharding import Mesh, PartitionSpec as P


W = 128
SLOTS = 16
HALF = SLOTS // 2
CHUNK = 4
GT = 4
NXH, NXL, NZH, NZL, NYL = 2, 2, 4, 2, 2
GROUPS = (("xl", "zl", "yl", GT + 1), ("zl", "yl", "xl", GT), ("yl", "xl", "zl", GT))
F32 = jnp.float32
BF16 = jnp.bfloat16
ANY = pl.BlockSpec(memory_space=pl.ANY)
SMEM = pl.BlockSpec(memory_space=pltpu.SMEM)
VMEM = pl.BlockSpec(memory_space=pltpu.VMEM)
HBM = pl.BlockSpec(memory_space=pltpu.HBM)


def split(value):
    high = value.astype(BF16)
    return high, (value - high.astype(F32)).astype(BF16)


def camera_index():
    return lax.axis_index("yh") * 2 + lax.axis_index("c")


def cluster_device():
    xh, xl, zh, zl, yl = (lax.axis_index(name) for name in ("xh", "xl", "zh", "zl", "yl"))
    return (((xh * NXL + xl) * NZH + zh) * NZL + zl) * NYL + yl


def coupling_kernel(mine, pts_hbm, inv_ref, out_ref, pts_buf, sems):
    core = lax.axis_index("c")
    base = (core if mine else 1 - core) * HALF

    def fetch(i):
        return pltpu.make_async_copy(pts_hbm.at[base + i], pts_buf.at[i], sems.at[i])

    for i in range(HALF):
        fetch(i).start()
    for i in range(HALF):
        fetch(i).wait()
        pts = [pts_buf[i, j] for j in range(3)]
        pairs = []
        for k in range(3):
            weighted = None
            for j in range(3):
                term = pts[j] * inv_ref[j, k, pl.ds(base + i, 1), :]
                weighted = term if weighted is None else weighted + term
            pairs.append((split(weighted), split(pts[k])))
        left = jnp.concatenate([w[0] for w, _ in pairs] + [w[0] for w, _ in pairs] + [w[1] for w, _ in pairs], axis=1)
        right = jnp.concatenate([p[0] for _, p in pairs] + [p[1] for _, p in pairs] + [p[0] for _, p in pairs], axis=1)
        out_ref[i] = lax.dot_general(left, right, (((1,), (1,)), ((), ())), preferred_element_type=F32)


def coupling(mine, pts, inv):
    def kernel(*refs):
        coupling_kernel(mine, *refs)

    return pl.pallas_call(
        kernel,
        out_shape=jax.ShapeDtypeStruct((HALF, W, W), F32),
        in_specs=[HBM, VMEM],
        out_specs=VMEM,
        scratch_shapes=[pltpu.VMEM((HALF, 3, W, W), F32), pltpu.SemaphoreType.DMA((HALF,))],
        cost_estimate=pl.CostEstimate(flops=HALF * 2 * 9 * W * W * W, bytes_accessed=HALF * 4 * W * W * 4, transcendentals=0),
        compiler_params=pltpu.CompilerParams(vmem_limit_bytes=8 << 20),
        name="coupling",
    )(pts, inv)


def schur_kernel(counts_ref, tiles_ref, own_ref, oth_ref, c0_ref, c1_ref, c2_ref, c3_ref, *refs):
    outs, o_sems, accs = refs[:7], refs[7], refs[8:]
    core = lax.axis_index("c")
    cam = camera_index()
    device = cluster_device()
    live = counts_ref[device]
    panels = (c0_ref, c1_ref, c2_ref, c3_ref)

    steps = SLOTS // CHUNK
    for acc in accs:
        acc[...] = jnp.zeros_like(acc)

    for k in range(steps):
        @pl.when(k * CHUNK < live)
        def _():
            for i in range(CHUNK):
                slot = k * CHUNK + i
                m_high, m_low = split(jnp.where(core == k // 2, own_ref[slot % HALF], oth_ref[slot % HALF]))
                panel_t = c0_ref[slot].T
                t_high, t_low = split(panel_t)
                prod = jnp.dot(
                    jnp.concatenate([t_high, t_high, t_low], axis=1),
                    jnp.concatenate([m_high, m_low, m_high], axis=0),
                    preferred_element_type=F32,
                )
                rest = panel_t - prod
                if i:
                    rest = jnp.where(slot < live, rest, 0.0)
                r_high, r_low = split(rest)
                left = jnp.concatenate([r_high, r_high, r_low], axis=1)
                parts = [split(panels[rel][slot]) for rel in range(4)]
                highs = jnp.concatenate([h for h, _ in parts], axis=1)
                lows = jnp.concatenate([l for _, l in parts], axis=1)
                right = jnp.concatenate([highs, lows, highs], axis=0)
                rows = jnp.dot(left, right, preferred_element_type=F32)
                row_tile = tiles_ref[cam, device * SLOTS + slot]
                for rel in range(4):
                    block = rows[:, rel * W : (rel + 1) * W].reshape(NZH, NZL, NYL, 8, W)

                    def add(group, tile, block=block):
                        for zl in range(NZL):
                            for yl in range(NYL):
                                at = {"xl": lax.rem(row_tile, NXL), "zl": zl, "yl": yl}
                                lead = tuple(at[name] for name in GROUPS[group][:3])
                                accs[group][lead + (row_tile // NXL, slice(None), tile)] += block[:, zl, yl]

                    if rel == 0:
                        add(0, GT)
                        continue
                    tile = tiles_ref[lax.bitwise_xor(cam, rel), device * SLOTS + slot]
                    add(rel - 1, tile)

    copies = []
    for group, names in enumerate(GROUPS):
        bit = lax.axis_index(names[0])
        away = accs[group].at[1 - bit]
        copies += [away.at[0], away.at[1]] if group == 0 else [away]
        copies.append(accs[group].at[bit])
    copies = [pltpu.make_async_copy(source, outs[k], o_sems.at[k]) for k, source in enumerate(copies)]
    for copy in copies:
        copy.start()
    for copy in copies:
        copy.wait()


def schur(counts, tiles, own, oth, panels):
    return pl.pallas_call(
        schur_kernel,
        out_shape=[
            jax.ShapeDtypeStruct(lead + (2, NXH, NZH, names[3], 8, W), F32) for k, names in enumerate(GROUPS)
            for lead in (((), (), (2,)) if k == 0 else ((2,), (2,)))
        ],
        in_specs=[SMEM, SMEM] + [VMEM] * 6,
        out_specs=[ANY] * 7,
        scratch_shapes=[
            pltpu.SemaphoreType.DMA((7,)),
        ]
        + [pltpu.VMEM((2, 2, 2, NXH, NZH, names[3], 8, W), F32) for names in GROUPS],
        cost_estimate=pl.CostEstimate(flops=SLOTS * 6 * 5 * W * W * W, bytes_accessed=SLOTS * 5 * W * W * 4, transcendentals=0),
        compiler_params=pltpu.CompilerParams(vmem_limit_bytes=12 << 20),
        name="schur",
    )(counts, tiles, *[pltpu.with_memory_space_constraint(v, pltpu.VMEM) for v in (own, oth, *panels)])


def place_kernel(in_ref, out_ref):
    cam = camera_index()
    x = lax.axis_index("xh") * NXL + lax.axis_index("xl")
    out_ref[...] = jnp.zeros_like(out_ref)

    def total(tile):
        value = in_ref[0, tile]
        for source in range(1, NXH * NZH):
            value = value + in_ref[source, tile]
        return value

    row = 0
    for rel, t in [(1, t) for t in range(GT)] + [(0, x)] + [(rel, t) for rel in (2, 3) for t in range(GT)]:
        column = lax.bitwise_xor(cam, rel) * GT + t
        out_ref[0, :, pl.ds(pl.multiple_of(column * W, W), W)] = total(row)
        row += 1


def place(pieces):
    return pl.pallas_call(
        place_kernel,
        out_shape=jax.ShapeDtypeStruct((1, 8, 4 * GT * W), F32),
        in_specs=[VMEM],
        out_specs=VMEM,
        compiler_params=pltpu.CompilerParams(vmem_limit_bytes=4 << 20),
        name="place",
    )(pieces)


def halve_kernel(axis, keep_ref, *refs):
    parts, send_ref, out_ref = refs[:-2], refs[-2], refs[-1]
    bit = lax.axis_index(axis)
    for at in range(2):
        value = keep_ref[at] + (parts[at][...] if len(parts) == 2 else parts[0][at])

        @pl.when(bit == at)
        def _():
            out_ref[...] = value

        @pl.when(bit != at)
        def _():
            send_ref[...] = value


def halve(axis, keep, parts):
    def kernel(*refs):
        halve_kernel(axis, *refs)

    return pl.pallas_call(
        kernel,
        out_shape=[jax.ShapeDtypeStruct(keep.shape[1:], F32)] * 2,
        in_specs=[VMEM] * (1 + len(parts)),
        out_specs=[VMEM] * 2,
        compiler_params=pltpu.CompilerParams(vmem_limit_bytes=4 << 20),
        name="halve",
    )(*[pltpu.with_memory_space_constraint(v, pltpu.VMEM) for v in (keep, *parts)])


def swap_x_other(value):
    size = NXH * NXL
    return lax.ppermute(value, ("xh", "xl"), [(i, (i + 1 if i % 2 else i - 1) % size) for i in range(size)])


def swap(value, axis):
    return lax.ppermute(value, axis, [(0, 1), (1, 0)])


def on_device(counts, tiles, cam_jac, point_jac, point_inv):
    pts = point_jac.transpose(0, 2, 1, 3)
    inv = point_inv.transpose(1, 2, 0, 3)

    c0 = cam_jac
    c2 = swap(c0, "yh")
    c1 = swap(c0, "c")

    m_send = coupling(False, pts, inv)
    m_recv = swap(m_send, "c")
    m_keep = coupling(True, pts, inv)
    m_chip = m_keep + m_recv
    m_own = m_chip + swap(m_chip, "yh")
    m_oth = swap(m_own, "c")
    c3 = swap(c2, "c")

    outs = schur(counts, tiles.T, m_own, m_oth, (c0, c1, c2, c3))
    near_z = swap(outs[3], "zl")
    near_y = swap(outs[5], "yl")
    low_x = swap(outs[0], "xl")
    high_x = swap_x_other(outs[1])
    groups = [(outs[2], (low_x, high_x)), (outs[4], (near_z,)), (outs[6], (near_y,))]
    for phase in (1, 2):
        halves = []
        for k, (keep, parts) in enumerate(groups):
            halves.append(halve(GROUPS[k][phase], keep, parts))
        groups = []
        for k, (send, keep) in enumerate(halves):
            groups.append((keep, (swap(send, GROUPS[k][phase]),)))
    groups = [(keep, parts[0]) for keep, parts in groups]
    received = [got for _, got in groups]
    part = jnp.concatenate(
        [(keep + got).reshape(NXH * NZH, -1, 8, W) for (keep, _), got in zip(groups, received)], axis=1
    )
    return place(lax.all_to_all(part, ("xh", "zh"), 0, 0, tiled=True))


def solution(mesh):
    fine = Mesh(mesh.devices.reshape(NXH, NXL, NZH, NZL, NYL, 2, 2), ("xh", "xl", "zh", "zl", "yl", "yh", "c"))
    rows = ("xh", "xl", "zh", "zl", "yl")
    cams = ("yh", "c")
    in_specs = (
        P(),
        P(),
        P(rows, None, cams),
        P(rows, None, None, cams),
        P(rows, None, None, cams),
    )
    return jax.shard_map(
        on_device, mesh=fine, in_specs=in_specs, out_specs=P(cams, rows, None), check_vma=False
    )
```

```python
import itertools

import jax
import jax.numpy as jnp
from jax import lax
from jax.experimental import pallas as pl
from jax.experimental.pallas import tpu as pltpu
from jax.sharding import Mesh, PartitionSpec as P


W = 128
SLOTS = 16
HALF = SLOTS // 2
CHUNK = 4
GT = 4
NXH, NXL, NZA, NZB, NZL, NYL = 2, 2, 2, 2, 2, 2
TILES = (GT + 1, GT, GT)
AXES = (
    ("xl", "zl", "yl", "xh", "zb", "za"),
    ("zl", "yl", "xl", "zb", "za", "xh"),
    ("yl", "xl", "zl", "za", "xh", "zb"),
)
PHASES = 6
ROWS = ("xh", "xl", "za", "zb", "zl", "yl")
F32 = jnp.float32
BF16 = jnp.bfloat16
ANY = pl.BlockSpec(memory_space=pl.ANY)
SMEM = pl.BlockSpec(memory_space=pltpu.SMEM)
VMEM = pl.BlockSpec(memory_space=pltpu.VMEM)
HBM = pl.BlockSpec(memory_space=pltpu.HBM)


def split(value):
    high = value.astype(BF16)
    return high, (value - high.astype(F32)).astype(BF16)


def camera_index():
    return lax.axis_index("yh") * 2 + lax.axis_index("c")


def cluster_device():
    index = 0
    for name in ROWS:
        index = index * 2 + lax.axis_index(name)
    return index


def coupling_kernel(mine, pts_hbm, inv_ref, out_ref, pts_buf, sems):
    core = lax.axis_index("c")
    base = (core if mine else 1 - core) * HALF

    def fetch(i):
        return pltpu.make_async_copy(pts_hbm.at[base + i], pts_buf.at[i], sems.at[i])

    for i in range(HALF):
        fetch(i).start()
    for i in range(HALF):
        fetch(i).wait()
        pts = [pts_buf[i, j] for j in range(3)]
        pairs = []
        for k in range(3):
            weighted = None
            for j in range(3):
                term = pts[j] * inv_ref[j, k, pl.ds(base + i, 1), :]
                weighted = term if weighted is None else weighted + term
            pairs.append((split(weighted), split(pts[k])))
        left = jnp.concatenate([w[0] for w, _ in pairs] + [w[0] for w, _ in pairs] + [w[1] for w, _ in pairs], axis=1)
        right = jnp.concatenate([p[0] for _, p in pairs] + [p[1] for _, p in pairs] + [p[0] for _, p in pairs], axis=1)
        out_ref[i] = lax.dot_general(left, right, (((1,), (1,)), ((), ())), preferred_element_type=F32)


def coupling(mine, pts, inv):
    def kernel(*refs):
        coupling_kernel(mine, *refs)

    return pl.pallas_call(
        kernel,
        out_shape=jax.ShapeDtypeStruct((HALF, W, W), F32),
        in_specs=[HBM, VMEM],
        out_specs=VMEM,
        scratch_shapes=[pltpu.VMEM((HALF, 3, W, W), F32), pltpu.SemaphoreType.DMA((HALF,))],
        cost_estimate=pl.CostEstimate(flops=HALF * 2 * 9 * W * W * W, bytes_accessed=HALF * 4 * W * W * 4, transcendentals=0),
        compiler_params=pltpu.CompilerParams(vmem_limit_bytes=8 << 20),
        name="coupling",
    )(pts, inv)


def schur_kernel(counts_ref, tiles_ref, own_ref, oth_ref, c0_ref, c1_ref, c2_ref, c3_ref, *refs):
    outs, o_sems, accs = refs[:7], refs[7], refs[8:]
    core = lax.axis_index("c")
    cam = camera_index()
    device = cluster_device()
    live = counts_ref[device]
    panels = (c0_ref, c1_ref, c2_ref, c3_ref)

    steps = SLOTS // CHUNK
    for acc in accs:
        acc[...] = jnp.zeros_like(acc)

    for k in range(steps):
        @pl.when(k * CHUNK < live)
        def _():
            for i in range(CHUNK):
                slot = k * CHUNK + i
                m_high, m_low = split(jnp.where(core == k // 2, own_ref[slot % HALF], oth_ref[slot % HALF]))
                panel_t = c0_ref[slot].T
                t_high, t_low = split(panel_t)
                prod = jnp.dot(
                    jnp.concatenate([t_high, t_high, t_low], axis=1),
                    jnp.concatenate([m_high, m_low, m_high], axis=0),
                    preferred_element_type=F32,
                )
                rest = panel_t - prod
                if i:
                    rest = jnp.where(slot < live, rest, 0.0)
                r_high, r_low = split(rest)
                left = jnp.concatenate([r_high, r_high, r_low], axis=1)
                parts = [split(panels[rel][slot]) for rel in range(4)]
                highs = jnp.concatenate([h for h, _ in parts], axis=1)
                lows = jnp.concatenate([l for _, l in parts], axis=1)
                right = jnp.concatenate([highs, lows, highs], axis=0)
                rows = jnp.dot(left, right, preferred_element_type=F32)
                row_tile = tiles_ref[cam, device * SLOTS + slot]
                for rel in range(4):
                    block = rows[:, rel * W : (rel + 1) * W].reshape(NZA, NZB, NZL, NYL, 8, W)

                    def add(group, tile, block=block):
                        for za, zb, zl, yl in itertools.product(range(2), repeat=4):
                            at = {"xl": lax.rem(row_tile, NXL), "xh": row_tile // NXL, "za": za, "zb": zb, "zl": zl, "yl": yl}
                            accs[group][tuple(at[name] for name in AXES[group]) + (tile,)] += block[za, zb, zl, yl]

                    if rel == 0:
                        add(0, GT)
                        continue
                    tile = tiles_ref[lax.bitwise_xor(cam, rel), device * SLOTS + slot]
                    add(rel - 1, tile)

    copies = []
    for group, names in enumerate(AXES):
        bit = lax.axis_index(names[0])
        away = accs[group].at[1 - bit]
        copies += [away.at[0], away.at[1]] if group == 0 else [away]
        copies.append(accs[group].at[bit])
    copies = [pltpu.make_async_copy(source, outs[k], o_sems.at[k]) for k, source in enumerate(copies)]
    for copy in copies:
        copy.start()
    for copy in copies:
        copy.wait()


def schur(counts, tiles, own, oth, panels):
    return pl.pallas_call(
        schur_kernel,
        out_shape=[
            jax.ShapeDtypeStruct(lead + (2,) * (PHASES - 2) + (count, 8, W), F32)
            for k, count in enumerate(TILES)
            for lead in (((), (), (2,)) if k == 0 else ((2,), (2,)))
        ],
        in_specs=[SMEM, SMEM] + [VMEM] * 6,
        out_specs=[ANY] * 7,
        scratch_shapes=[
            pltpu.SemaphoreType.DMA((7,)),
        ]
        + [pltpu.VMEM((2,) * PHASES + (count, 8, W), F32) for count in TILES],
        cost_estimate=pl.CostEstimate(flops=SLOTS * 6 * 5 * W * W * W, bytes_accessed=SLOTS * 5 * W * W * 4, transcendentals=0),
        compiler_params=pltpu.CompilerParams(vmem_limit_bytes=12 << 20),
        name="schur",
    )(counts, tiles, *[pltpu.with_memory_space_constraint(v, pltpu.VMEM) for v in (own, oth, *panels)])


def place_kernel(*refs):
    out_ref = refs[-1]
    cam = camera_index()
    x = lax.axis_index("xh") * NXL + lax.axis_index("xl")
    out_ref[...] = jnp.zeros_like(out_ref)
    for rel in range(4):
        for t in [x] if rel == 0 else range(GT):
            group, tile = (0, GT) if rel == 0 else (rel - 1, t)
            column = lax.bitwise_xor(cam, rel) * GT + t
            value = refs[group * 2][tile] + refs[group * 2 + 1][tile]
            out_ref[0, :, pl.ds(pl.multiple_of(column * W, W), W)] = value


def place(pieces):
    return pl.pallas_call(
        place_kernel,
        out_shape=jax.ShapeDtypeStruct((1, 8, 4 * GT * W), F32),
        in_specs=[VMEM] * len(pieces),
        out_specs=VMEM,
        compiler_params=pltpu.CompilerParams(vmem_limit_bytes=4 << 20),
        name="place",
    )(*[pltpu.with_memory_space_constraint(v, pltpu.VMEM) for v in pieces])


def halve_kernel(axis, keep_ref, *refs):
    parts, send_ref, out_ref = refs[:-2], refs[-2], refs[-1]
    bit = lax.axis_index(axis)
    for at in range(2):
        value = keep_ref[at] + (parts[at][...] if len(parts) == 2 else parts[0][at])

        @pl.when(bit == at)
        def _():
            out_ref[...] = value

        @pl.when(bit != at)
        def _():
            send_ref[...] = value


def halve(axis, keep, parts):
    def kernel(*refs):
        halve_kernel(axis, *refs)

    return pl.pallas_call(
        kernel,
        out_shape=[jax.ShapeDtypeStruct(keep.shape[1:], F32)] * 2,
        in_specs=[VMEM] * (1 + len(parts)),
        out_specs=[VMEM] * 2,
        compiler_params=pltpu.CompilerParams(vmem_limit_bytes=4 << 20),
        name="halve",
    )(*[pltpu.with_memory_space_constraint(v, pltpu.VMEM) for v in (keep, *parts)])


def swap_x_other(value):
    size = NXH * NXL
    return lax.ppermute(value, ("xh", "xl"), [(i, (i + 1 if i % 2 else i - 1) % size) for i in range(size)])


def swap(value, axis):
    return lax.ppermute(value, axis, [(0, 1), (1, 0)])


def on_device(counts, tiles, cam_jac, point_jac, point_inv):
    pts = point_jac.transpose(0, 2, 1, 3)
    inv = point_inv.transpose(1, 2, 0, 3)

    c0 = cam_jac
    c2 = swap(c0, "yh")
    c1 = swap(c0, "c")

    m_send = coupling(False, pts, inv)
    m_recv = swap(m_send, "c")
    m_keep = coupling(True, pts, inv)
    m_chip = m_keep + m_recv
    m_own = m_chip + swap(m_chip, "yh")
    m_oth = swap(m_own, "c")
    c3 = swap(c2, "c")

    outs = schur(counts, tiles.T, m_own, m_oth, (c0, c1, c2, c3))
    near_z = swap(outs[3], "zl")
    near_y = swap(outs[5], "yl")
    low_x = swap(outs[0], "xl")
    high_x = swap_x_other(outs[1])
    groups = [(outs[2], (low_x, high_x)), (outs[4], (near_z,)), (outs[6], (near_y,))]
    for phase in range(1, PHASES):
        halves = []
        for k, (keep, parts) in enumerate(groups):
            halves.append(halve(AXES[k][phase], keep, parts))
        groups = []
        for k, (send, keep) in enumerate(halves):
            groups.append((keep, (swap(send, AXES[k][phase]),)))
    return place([piece for keep, parts in groups for piece in (keep, *parts)])


def solution(mesh):
    fine = Mesh(mesh.devices.reshape((2,) * 8), ROWS + ("yh", "c"))
    rows = ROWS
    cams = ("yh", "c")
    in_specs = (
        P(),
        P(),
        P(rows, None, cams),
        P(rows, None, None, cams),
        P(rows, None, None, cams),
    )
    return jax.shard_map(
        on_device, mesh=fine, in_specs=in_specs, out_specs=P(cams, rows, None), check_vma=False
    )
```

```python
import jax
import jax.numpy as jnp
from jax import lax
from jax.experimental import pallas as pl
from jax.experimental.pallas import tpu as pltpu
from jax.sharding import Mesh, PartitionSpec as P


W = 128
SLOTS = 16
BASE = 8
MOVED = 4
CAP = BASE + MOVED
HALF = CAP // 2
CHUNK = 4
GT = 4
PARTNER = 32
NXH, NXL, NZH, NZL, NYL = 2, 2, 4, 2, 2
GROUPS = (("xl", "zl", "yl", GT + 1), ("zl", "yl", "xl", GT), ("yl", "xl", "zl", GT))
F32 = jnp.float32
BF16 = jnp.bfloat16
ANY = pl.BlockSpec(memory_space=pl.ANY)
SMEM = pl.BlockSpec(memory_space=pltpu.SMEM)
VMEM = pl.BlockSpec(memory_space=pltpu.VMEM)
HBM = pl.BlockSpec(memory_space=pltpu.HBM)


COUPLING_MIB = 8


def split(value):
    high = value.astype(BF16)
    return high, (value - high.astype(F32)).astype(BF16)


def camera_index():
    return lax.axis_index("yh") * 2 + lax.axis_index("c")


def cluster_device():
    xh, xl, zh, zl, yl = (lax.axis_index(name) for name in ("xh", "xl", "zh", "zl", "yl"))
    return (((xh * NXL + xl) * NZH + zh) * NZL + zl) * NYL + yl


def half_slots(half):
    return [half * (BASE // 2) + i for i in range(BASE // 2)] + [BASE + half * (MOVED // 2) + i for i in range(MOVED // 2)]


def coupling_kernel(which, pts_hbm, inv_ref, out_ref, pts_buf, sems):
    core = lax.axis_index("c")
    if which == "moved":
        slots = [CAP + i for i in range(MOVED)]
    else:
        slots = half_slots(core if which == "keep" else 1 - core)

    copies = [pltpu.make_async_copy(pts_hbm.at[slot], pts_buf.at[i], sems.at[i]) for i, slot in enumerate(slots)]
    for copy in copies:
        copy.start()
    for i, slot in enumerate(slots):
        copies[i].wait()
        pts = [pts_buf[i, j] for j in range(3)]
        pairs = []
        for k in range(3):
            weighted = None
            for j in range(3):
                term = pts[j] * inv_ref[j, k, pl.ds(slot, 1), :]
                weighted = term if weighted is None else weighted + term
            pairs.append((split(weighted), split(pts[k])))
        left = jnp.concatenate([w[0] for w, _ in pairs] + [w[0] for w, _ in pairs] + [w[1] for w, _ in pairs], axis=1)
        right = jnp.concatenate([p[0] for _, p in pairs] + [p[1] for _, p in pairs] + [p[0] for _, p in pairs], axis=1)
        out_ref[i] = lax.dot_general(left, right, (((1,), (1,)), ((), ())), preferred_element_type=F32)


def coupling(which, pts, inv):
    count = MOVED if which == "moved" else HALF

    def kernel(*refs):
        coupling_kernel(which, *refs)

    return pl.pallas_call(
        kernel,
        out_shape=jax.ShapeDtypeStruct((count, W, W), F32),
        in_specs=[HBM, VMEM],
        out_specs=VMEM,
        scratch_shapes=[pltpu.VMEM((count, 3, W, W), F32), pltpu.SemaphoreType.DMA((count,))],
        cost_estimate=pl.CostEstimate(flops=count * 2 * 9 * W * W * W, bytes_accessed=count * 4 * W * W * 4, transcendentals=0),
        compiler_params=pltpu.CompilerParams(vmem_limit_bytes=COUPLING_MIB << 20),
        name="coupling",
    )(pts, inv)


def combine_kernel(counts_ref, keep_ref, recv_ref, mine_ref, other_ref, out_ref):
    core = lax.axis_index("c")
    heavy = counts_ref[cluster_device()] > CAP
    for i in range(HALF):
        value = keep_ref[i] + recv_ref[i]
        if i >= BASE // 2:
            at = core * (MOVED // 2) + i - BASE // 2
            value = jnp.where(heavy, value, mine_ref[at] + other_ref[at])
        out_ref[i] = value


def in_vmem(values):
    return [pltpu.with_memory_space_constraint(v, pltpu.VMEM) for v in values]


def combine(counts, *values):
    return pl.pallas_call(
        combine_kernel,
        out_shape=jax.ShapeDtypeStruct((HALF, W, W), F32),
        in_specs=[SMEM] + [VMEM] * 4,
        out_specs=VMEM,
        compiler_params=pltpu.CompilerParams(vmem_limit_bytes=4 << 20),
        name="combine",
    )(counts, *in_vmem(values))


def choose_kernel(counts_ref, own_ref, recv_ref, out_ref):
    heavy = counts_ref[cluster_device()] > CAP
    out_ref[...] = jnp.where(heavy, own_ref[...], recv_ref[...])


def choose(counts, own, recv):
    return pl.pallas_call(
        choose_kernel,
        out_shape=jax.ShapeDtypeStruct(own.shape, F32),
        in_specs=[SMEM] + [VMEM] * 2,
        out_specs=VMEM,
        compiler_params=pltpu.CompilerParams(vmem_limit_bytes=4 << 20),
        name="choose",
    )(counts, *in_vmem((own, recv)))


def schur_kernel(counts_ref, tiles_ref, own_ref, oth_ref, *refs):
    base_panels, moved_panels, outs, o_sems, accs = refs[:4], refs[4:8], refs[8:15], refs[15], refs[16:]
    core = lax.axis_index("c")
    cam = camera_index()
    device = cluster_device()
    count = counts_ref[device]
    partner = lax.bitwise_xor(device, PARTNER)
    heavy = count > CAP
    moved_live = jnp.where(heavy, count - BASE, counts_ref[partner] - CAP)
    moved_first = jnp.where(heavy, device * SLOTS + BASE, partner * SLOTS + CAP)

    for acc in accs:
        acc[...] = jnp.zeros_like(acc)

    for k in range(CAP // CHUNK):
        moved = k * CHUNK >= BASE
        panels = moved_panels if moved else base_panels
        start = k * CHUNK - (BASE if moved else 0)
        live = moved_live if moved else count

        @pl.when(start < live)
        def _():
            for i in range(CHUNK):
                slot = start + i
                table = (moved_first if moved else device * SLOTS) + slot
                per_half = (MOVED if moved else BASE) // 2
                m_at = slot % per_half + (BASE // 2 if moved else 0)
                m_high, m_low = split(jnp.where(core == slot // per_half, own_ref[m_at], oth_ref[m_at]))
                panel_t = panels[0][slot].T
                t_high, t_low = split(panel_t)
                prod = jnp.dot(
                    jnp.concatenate([t_high, t_high, t_low], axis=1),
                    jnp.concatenate([m_high, m_low, m_high], axis=0),
                    preferred_element_type=F32,
                )
                rest = panel_t - prod
                if i:
                    rest = jnp.where(slot < live, rest, 0.0)
                r_high, r_low = split(rest)
                left = jnp.concatenate([r_high, r_high, r_low], axis=1)
                parts = [split(panels[rel][slot]) for rel in range(4)]
                highs = jnp.concatenate([h for h, _ in parts], axis=1)
                lows = jnp.concatenate([l for _, l in parts], axis=1)
                right = jnp.concatenate([highs, lows, highs], axis=0)
                rows = jnp.dot(left, right, preferred_element_type=F32)
                row_tile = tiles_ref[cam, table]
                for rel in range(4):
                    block = rows[:, rel * W : (rel + 1) * W].reshape(NZH, NZL, NYL, 8, W)

                    def add(group, tile, block=block):
                        for zl in range(NZL):
                            for yl in range(NYL):
                                at = {"xl": lax.rem(row_tile, NXL), "zl": zl, "yl": yl}
                                lead = tuple(at[name] for name in GROUPS[group][:3])
                                accs[group][lead + (row_tile // NXL, slice(None), tile)] += block[:, zl, yl]

                    if rel == 0:
                        add(0, GT)
                        continue
                    tile = tiles_ref[lax.bitwise_xor(cam, rel), table]
                    add(rel - 1, tile)

    copies = []
    for group, names in enumerate(GROUPS):
        bit = lax.axis_index(names[0])
        away = accs[group].at[1 - bit]
        copies += [away.at[0], away.at[1]] if group == 0 else [away]
        copies.append(accs[group].at[bit])
    copies = [pltpu.make_async_copy(source, outs[k], o_sems.at[k]) for k, source in enumerate(copies)]
    for copy in copies:
        copy.start()
    for copy in copies:
        copy.wait()


def schur(counts, tiles, own, oth, base_panels, moved_panels):
    return pl.pallas_call(
        schur_kernel,
        out_shape=[
            jax.ShapeDtypeStruct(lead + (2, NXH, NZH, names[3], 8, W), F32) for k, names in enumerate(GROUPS)
            for lead in (((), (), (2,)) if k == 0 else ((2,), (2,)))
        ],
        in_specs=[SMEM, SMEM] + [VMEM] * 10,
        out_specs=[ANY] * 7,
        scratch_shapes=[
            pltpu.SemaphoreType.DMA((7,)),
        ]
        + [pltpu.VMEM((2, 2, 2, NXH, NZH, names[3], 8, W), F32) for names in GROUPS],
        cost_estimate=pl.CostEstimate(flops=SLOTS * 6 * 5 * W * W * W, bytes_accessed=SLOTS * 5 * W * W * 4, transcendentals=0),
        compiler_params=pltpu.CompilerParams(vmem_limit_bytes=12 << 20),
        name="schur",
    )(counts, tiles, *in_vmem((own, oth, *base_panels, *moved_panels)))


def place_kernel(in_ref, out_ref):
    cam = camera_index()
    x = lax.axis_index("xh") * NXL + lax.axis_index("xl")
    out_ref[...] = jnp.zeros_like(out_ref)

    def total(tile):
        value = in_ref[0, tile]
        for source in range(1, NXH * NZH):
            value = value + in_ref[source, tile]
        return value

    row = 0
    for rel, t in [(1, t) for t in range(GT)] + [(0, x)] + [(rel, t) for rel in (2, 3) for t in range(GT)]:
        column = lax.bitwise_xor(cam, rel) * GT + t
        out_ref[0, :, pl.ds(pl.multiple_of(column * W, W), W)] = total(row)
        row += 1


def place(pieces):
    return pl.pallas_call(
        place_kernel,
        out_shape=jax.ShapeDtypeStruct((1, 8, 4 * GT * W), F32),
        in_specs=[VMEM],
        out_specs=VMEM,
        compiler_params=pltpu.CompilerParams(vmem_limit_bytes=4 << 20),
        name="place",
    )(pieces)


def halve_kernel(axis, keep_ref, *refs):
    parts, send_ref, out_ref = refs[:-2], refs[-2], refs[-1]
    bit = lax.axis_index(axis)
    for at in range(2):
        value = keep_ref[at] + (parts[at][...] if len(parts) == 2 else parts[0][at])

        @pl.when(bit == at)
        def _():
            out_ref[...] = value

        @pl.when(bit != at)
        def _():
            send_ref[...] = value


def halve(axis, keep, parts):
    def kernel(*refs):
        halve_kernel(axis, *refs)

    return pl.pallas_call(
        kernel,
        out_shape=[jax.ShapeDtypeStruct(keep.shape[1:], F32)] * 2,
        in_specs=[VMEM] * (1 + len(parts)),
        out_specs=[VMEM] * 2,
        compiler_params=pltpu.CompilerParams(vmem_limit_bytes=4 << 20),
        name="halve",
    )(*[pltpu.with_memory_space_constraint(v, pltpu.VMEM) for v in (keep, *parts)])


def swap_x_other(value):
    size = NXH * NXL
    return lax.ppermute(value, ("xh", "xl"), [(i, (i + 1 if i % 2 else i - 1) % size) for i in range(size)])


def swap(value, axis):
    return lax.ppermute(value, axis, [(0, 1), (1, 0)])


def on_device(counts, tiles, cam_jac, point_jac, point_inv):
    pts = point_jac.transpose(0, 2, 1, 3)
    inv = point_inv.transpose(1, 2, 0, 3)

    a0 = cam_jac[:BASE]
    a2 = swap(a0, "yh")
    b_recv = swap(cam_jac[CAP:], "xh")
    m_moved = coupling("moved", pts, inv)
    m_moved = swap(m_moved, "xh")
    m_recv = coupling("send", pts, inv)
    m_recv = swap(m_recv, "c")
    b0 = choose(counts, cam_jac[BASE:CAP], b_recv)
    b2 = swap(b0, "yh")
    m_keep = coupling("keep", pts, inv)
    m_chip = combine(counts, m_keep, m_recv, m_moved, swap(m_moved, "c"))
    m_own = m_chip + swap(m_chip, "yh")
    m_oth = swap(m_own, "c")
    base = (a0, swap(a0, "c"), a2, swap(a2, "c"))
    moved = (b0, swap(b0, "c"), b2, swap(b2, "c"))
    outs = schur(counts, tiles.T, m_own, m_oth, base, moved)
    near_z = swap(outs[3], "zl")
    near_y = swap(outs[5], "yl")
    low_x = swap(outs[0], "xl")
    high_x = swap_x_other(outs[1])
    groups = [(outs[2], (low_x, high_x)), (outs[4], (near_z,)), (outs[6], (near_y,))]
    for phase in (1, 2):
        halves = []
        for k, (keep, parts) in enumerate(groups):
            halves.append(halve(GROUPS[k][phase], keep, parts))
        groups = []
        for k, (send, keep) in enumerate(halves):
            groups.append((keep, (swap(send, GROUPS[k][phase]),)))
    groups = [(keep, parts[0]) for keep, parts in groups]
    received = [got for _, got in groups]
    part = jnp.concatenate(
        [(keep + got).reshape(NXH * NZH, -1, 8, W) for (keep, _), got in zip(groups, received)], axis=1
    )
    return place(lax.all_to_all(part, ("xh", "zh"), 0, 0, tiled=True))


def solution(mesh):
    fine = Mesh(mesh.devices.reshape(NXH, NXL, NZH, NZL, NYL, 2, 2), ("xh", "xl", "zh", "zl", "yl", "yh", "c"))
    rows = ("xh", "xl", "zh", "zl", "yl")
    cams = ("yh", "c")
    in_specs = (
        P(),
        P(),
        P(rows, None, cams),
        P(rows, None, None, cams),
        P(rows, None, None, cams),
    )
    return jax.shard_map(
        on_device, mesh=fine, in_specs=in_specs, out_specs=P(cams, rows, None), check_vma=False
    )
```

```python
import jax
import jax.numpy as jnp
from jax import lax
from jax.experimental import pallas as pl
from jax.experimental.pallas import tpu as pltpu
from jax.sharding import Mesh, PartitionSpec as P


W = 128
SLOTS = 16
HALF = SLOTS // 2
CHUNK = 4
GT = 4
NXH, NXL, NZH, NZL, NYL = 2, 2, 4, 2, 2
GROUPS = (("xl", "zl", "yl", GT + 1), ("zl", "yl", "xl", GT), ("yl", "xl", "zl", GT))
F32 = jnp.float32
BF16 = jnp.bfloat16
ANY = pl.BlockSpec(memory_space=pl.ANY)
SMEM = pl.BlockSpec(memory_space=pltpu.SMEM)
VMEM = pl.BlockSpec(memory_space=pltpu.VMEM)
HBM = pl.BlockSpec(memory_space=pltpu.HBM)


def split(value):
    high = value.astype(BF16)
    return high, (value - high.astype(F32)).astype(BF16)


def camera_index():
    return lax.axis_index("yh") * 2 + lax.axis_index("c")


def cluster_device():
    xh, xl, zh, zl, yl = (lax.axis_index(name) for name in ("xh", "xl", "zh", "zl", "yl"))
    return (((xh * NXL + xl) * NZH + zh) * NZL + zl) * NYL + yl


def coupling_kernel(mine, pts_hbm, inv_ref, out_ref, pts_buf, sems):
    core = lax.axis_index("c")
    base = (core if mine else 1 - core) * HALF

    def fetch(i):
        return pltpu.make_async_copy(pts_hbm.at[base + i], pts_buf.at[i], sems.at[i])

    for i in range(HALF):
        fetch(i).start()
    for i in range(HALF):
        fetch(i).wait()
        pts = [pts_buf[i, j] for j in range(3)]
        pairs = []
        for k in range(3):
            weighted = None
            for j in range(3):
                term = pts[j] * inv_ref[j, k, pl.ds(base + i, 1), :]
                weighted = term if weighted is None else weighted + term
            pairs.append((split(weighted), split(pts[k])))
        left = jnp.concatenate([w[0] for w, _ in pairs] + [w[0] for w, _ in pairs] + [w[1] for w, _ in pairs], axis=1)
        right = jnp.concatenate([p[0] for _, p in pairs] + [p[1] for _, p in pairs] + [p[0] for _, p in pairs], axis=1)
        out_ref[i] = lax.dot_general(left, right, (((1,), (1,)), ((), ())), preferred_element_type=F32)


def coupling(mine, pts, inv):
    def kernel(*refs):
        coupling_kernel(mine, *refs)

    return pl.pallas_call(
        kernel,
        out_shape=jax.ShapeDtypeStruct((HALF, W, W), F32),
        in_specs=[HBM, VMEM],
        out_specs=VMEM,
        scratch_shapes=[pltpu.VMEM((HALF, 3, W, W), F32), pltpu.SemaphoreType.DMA((HALF,))],
        cost_estimate=pl.CostEstimate(flops=HALF * 2 * 9 * W * W * W, bytes_accessed=HALF * 4 * W * W * 4, transcendentals=0),
        compiler_params=pltpu.CompilerParams(vmem_limit_bytes=8 << 20),
        name="coupling",
    )(pts, inv)


def prepare_kernel(counts_ref, c0_ref, c1_ref, c2_ref, c3_ref, high_ref, low_ref, t_ref, t_high_ref, t_low_ref):
    live = counts_ref[cluster_device()]
    for k in range(SLOTS // CHUNK):

        @pl.when(k * CHUNK < live)
        def _():
            for slot in range(k * CHUNK, (k + 1) * CHUNK):
                for rel, ref in enumerate((c0_ref, c1_ref, c2_ref, c3_ref)):
                    high, low = split(ref[slot])
                    high_ref[slot, :, rel * W : (rel + 1) * W] = high
                    low_ref[slot, :, rel * W : (rel + 1) * W] = low
                panel_t = c0_ref[slot].T
                t_ref[slot] = panel_t
                t_high_ref[slot], t_low_ref[slot] = split(panel_t)


def in_vmem(values):
    return [pltpu.with_memory_space_constraint(v, pltpu.VMEM) for v in values]


def prepare(counts, panels):
    wide, square = (SLOTS, W, 4 * W), (SLOTS, W, W)
    return pl.pallas_call(
        prepare_kernel,
        out_shape=[
            jax.ShapeDtypeStruct(shape, kind)
            for shape, kind in ((wide, BF16), (wide, BF16), (square, F32), (square, BF16), (square, BF16))
        ],
        in_specs=[SMEM] + [VMEM] * 4,
        out_specs=[VMEM] * 5,
        cost_estimate=pl.CostEstimate(flops=SLOTS * 20 * W * W, bytes_accessed=SLOTS * 12 * W * W * 4, transcendentals=0),
        compiler_params=pltpu.CompilerParams(vmem_limit_bytes=8 << 20),
        name="prepare",
    )(counts, *in_vmem(panels))


def schur_kernel(counts_ref, tiles_ref, own_ref, oth_ref, high_ref, low_ref, t_ref, t_high_ref, t_low_ref, *refs):
    outs, o_sems, accs = refs[:7], refs[7], refs[8:]
    core = lax.axis_index("c")
    cam = camera_index()
    device = cluster_device()
    live = counts_ref[device]
    steps = SLOTS // CHUNK
    for acc in accs:
        acc[...] = jnp.zeros_like(acc)

    for k in range(steps):
        @pl.when(k * CHUNK < live)
        def _():
            for i in range(CHUNK):
                slot = k * CHUNK + i
                m_high, m_low = split(jnp.where(core == k // 2, own_ref[slot % HALF], oth_ref[slot % HALF]))
                t_high, t_low = t_high_ref[slot], t_low_ref[slot]
                prod = jnp.dot(
                    jnp.concatenate([t_high, t_high, t_low], axis=1),
                    jnp.concatenate([m_high, m_low, m_high], axis=0),
                    preferred_element_type=F32,
                )
                rest = t_ref[slot] - prod
                if i:
                    rest = jnp.where(slot < live, rest, 0.0)
                r_high, r_low = split(rest)
                left = jnp.concatenate([r_high, r_high, r_low], axis=1)
                highs = high_ref[slot]
                right = jnp.concatenate([highs, low_ref[slot], highs], axis=0)
                rows = jnp.dot(left, right, preferred_element_type=F32)
                row_tile = tiles_ref[cam, device * SLOTS + slot]
                for rel in range(4):
                    block = rows[:, rel * W : (rel + 1) * W].reshape(NZH, NZL, NYL, 8, W)

                    def add(group, tile, block=block):
                        for zl in range(NZL):
                            for yl in range(NYL):
                                at = {"xl": lax.rem(row_tile, NXL), "zl": zl, "yl": yl}
                                lead = tuple(at[name] for name in GROUPS[group][:3])
                                accs[group][lead + (row_tile // NXL, slice(None), tile)] += block[:, zl, yl]

                    if rel == 0:
                        add(0, GT)
                        continue
                    tile = tiles_ref[lax.bitwise_xor(cam, rel), device * SLOTS + slot]
                    add(rel - 1, tile)

    copies = []
    for group, names in enumerate(GROUPS):
        bit = lax.axis_index(names[0])
        away = accs[group].at[1 - bit]
        copies += [away.at[0], away.at[1]] if group == 0 else [away]
        copies.append(accs[group].at[bit])
    copies = [pltpu.make_async_copy(source, outs[k], o_sems.at[k]) for k, source in enumerate(copies)]
    for copy in copies:
        copy.start()
    for copy in copies:
        copy.wait()


def schur(counts, tiles, own, oth, ready):
    return pl.pallas_call(
        schur_kernel,
        out_shape=[
            jax.ShapeDtypeStruct(lead + (2, NXH, NZH, names[3], 8, W), F32) for k, names in enumerate(GROUPS)
            for lead in (((), (), (2,)) if k == 0 else ((2,), (2,)))
        ],
        in_specs=[SMEM, SMEM] + [VMEM] * 7,
        out_specs=[ANY] * 7,
        scratch_shapes=[
            pltpu.SemaphoreType.DMA((7,)),
        ]
        + [pltpu.VMEM((2, 2, 2, NXH, NZH, names[3], 8, W), F32) for names in GROUPS],
        cost_estimate=pl.CostEstimate(flops=SLOTS * 6 * 5 * W * W * W, bytes_accessed=SLOTS * 5 * W * W * 4, transcendentals=0),
        compiler_params=pltpu.CompilerParams(vmem_limit_bytes=12 << 20),
        name="schur",
    )(counts, tiles, *in_vmem((own, oth, *ready)))


def place_kernel(in_ref, out_ref):
    cam = camera_index()
    x = lax.axis_index("xh") * NXL + lax.axis_index("xl")
    out_ref[...] = jnp.zeros_like(out_ref)

    def total(tile):
        value = in_ref[0, tile]
        for source in range(1, NXH * NZH):
            value = value + in_ref[source, tile]
        return value

    row = 0
    for rel, t in [(1, t) for t in range(GT)] + [(0, x)] + [(rel, t) for rel in (2, 3) for t in range(GT)]:
        column = lax.bitwise_xor(cam, rel) * GT + t
        out_ref[0, :, pl.ds(pl.multiple_of(column * W, W), W)] = total(row)
        row += 1


def place(pieces):
    return pl.pallas_call(
        place_kernel,
        out_shape=jax.ShapeDtypeStruct((1, 8, 4 * GT * W), F32),
        in_specs=[VMEM],
        out_specs=VMEM,
        compiler_params=pltpu.CompilerParams(vmem_limit_bytes=4 << 20),
        name="place",
    )(pieces)


def halve_kernel(axis, keep_ref, *refs):
    parts, send_ref, out_ref = refs[:-2], refs[-2], refs[-1]
    bit = lax.axis_index(axis)
    for at in range(2):
        value = keep_ref[at] + (parts[at][...] if len(parts) == 2 else parts[0][at])

        @pl.when(bit == at)
        def _():
            out_ref[...] = value

        @pl.when(bit != at)
        def _():
            send_ref[...] = value


def halve(axis, keep, parts):
    def kernel(*refs):
        halve_kernel(axis, *refs)

    return pl.pallas_call(
        kernel,
        out_shape=[jax.ShapeDtypeStruct(keep.shape[1:], F32)] * 2,
        in_specs=[VMEM] * (1 + len(parts)),
        out_specs=[VMEM] * 2,
        compiler_params=pltpu.CompilerParams(vmem_limit_bytes=4 << 20),
        name="halve",
    )(*[pltpu.with_memory_space_constraint(v, pltpu.VMEM) for v in (keep, *parts)])


def swap_x_other(value):
    size = NXH * NXL
    return lax.ppermute(value, ("xh", "xl"), [(i, (i + 1 if i % 2 else i - 1) % size) for i in range(size)])


def swap(value, axis):
    return lax.ppermute(value, axis, [(0, 1), (1, 0)])


def on_device(counts, tiles, cam_jac, point_jac, point_inv):
    pts = point_jac.transpose(0, 2, 1, 3)
    inv = point_inv.transpose(1, 2, 0, 3)

    c0 = cam_jac
    c2 = swap(c0, "yh")
    c1 = swap(c0, "c")
    m_send = coupling(False, pts, inv)
    m_recv = swap(m_send, "c")
    m_keep = coupling(True, pts, inv)
    m_chip = m_keep + m_recv
    m_recv = swap(m_chip, "yh")
    c3 = swap(c2, "c")
    ready = prepare(counts, (c0, c1, c2, c3))
    m_own = m_chip + m_recv
    m_oth = swap(m_own, "c")
    outs = schur(counts, tiles.T, m_own, m_oth, ready)
    near_z = swap(outs[3], "zl")
    near_y = swap(outs[5], "yl")
    low_x = swap(outs[0], "xl")
    high_x = swap_x_other(outs[1])
    groups = [(outs[2], (low_x, high_x)), (outs[4], (near_z,)), (outs[6], (near_y,))]
    for phase in (1, 2):
        halves = []
        for k, (keep, parts) in enumerate(groups):
            halves.append(halve(GROUPS[k][phase], keep, parts))
        groups = []
        for k, (send, keep) in enumerate(halves):
            groups.append((keep, (swap(send, GROUPS[k][phase]),)))
    groups = [(keep, parts[0]) for keep, parts in groups]
    received = [got for _, got in groups]
    part = jnp.concatenate(
        [(keep + got).reshape(NXH * NZH, -1, 8, W) for (keep, _), got in zip(groups, received)], axis=1
    )
    return place(lax.all_to_all(part, ("xh", "zh"), 0, 0, tiled=True))


def solution(mesh):
    fine = Mesh(mesh.devices.reshape(NXH, NXL, NZH, NZL, NYL, 2, 2), ("xh", "xl", "zh", "zl", "yl", "yh", "c"))
    rows = ("xh", "xl", "zh", "zl", "yl")
    cams = ("yh", "c")
    in_specs = (
        P(),
        P(),
        P(rows, None, cams),
        P(rows, None, None, cams),
        P(rows, None, None, cams),
    )
    return jax.shard_map(
        on_device, mesh=fine, in_specs=in_specs, out_specs=P(cams, rows, None), check_vma=False
    )
```

```python
import jax
import jax.numpy as jnp
from jax import lax
from jax.experimental import pallas as pl
from jax.experimental.pallas import tpu as pltpu
from jax.sharding import Mesh, PartitionSpec as P


W = 128
SLOTS = 16
HALF = SLOTS // 2
CHUNK = 4
PACKED = 3 * W // 4
GT = 4
NXH, NXL, NZH, NZL, NYL = 2, 2, 4, 2, 2
GROUPS = (("xl", "zl", "yl", GT + 1), ("zl", "yl", "xl", GT + 1), ("yl", "xl", "zl", GT - 1))
F32 = jnp.float32
BF16 = jnp.bfloat16
ANY = pl.BlockSpec(memory_space=pl.ANY)
SMEM = pl.BlockSpec(memory_space=pltpu.SMEM)
VMEM = pl.BlockSpec(memory_space=pltpu.VMEM)
HBM = pl.BlockSpec(memory_space=pltpu.HBM)


def split(value):
    high = value.astype(BF16)
    return high, (value - high.astype(F32)).astype(BF16)


def camera_index():
    return lax.axis_index("yh") * 2 + lax.axis_index("c")


def cluster_device():
    xh, xl, zh, zl, yl = (lax.axis_index(name) for name in ("xh", "xl", "zh", "zl", "yl"))
    return (((xh * NXL + xl) * NZH + zh) * NZL + zl) * NYL + yl


def coupling_kernel(mine, pts_hbm, inv_ref, out_ref, pts_buf, sems):
    core = lax.axis_index("c")
    base = (core if mine else 1 - core) * HALF

    def fetch(i):
        return pltpu.make_async_copy(pts_hbm.at[base + i], pts_buf.at[i], sems.at[i])

    for i in range(HALF):
        fetch(i).start()
    for i in range(HALF):
        fetch(i).wait()
        pts = [pts_buf[i, j] for j in range(3)]
        pairs = []
        for k in range(3):
            weighted = None
            for j in range(3):
                term = pts[j] * inv_ref[j, k, pl.ds(base + i, 1), :]
                weighted = term if weighted is None else weighted + term
            pairs.append((split(weighted), split(pts[k])))
        left = jnp.concatenate([w[0] for w, _ in pairs] + [w[0] for w, _ in pairs] + [w[1] for w, _ in pairs], axis=1)
        right = jnp.concatenate([p[0] for _, p in pairs] + [p[1] for _, p in pairs] + [p[0] for _, p in pairs], axis=1)
        full = lax.dot_general(left, right, (((1,), (1,)), ((), ())), preferred_element_type=F32)
        out_ref[i, : W // 2] = full[: W // 2]
        out_ref[i, W // 2 :, : W // 2] = full[W // 2 : PACKED, W // 2 :]
        out_ref[i, W // 2 :, W // 2 :] = full[PACKED:, W // 2 :]


def coupling(mine, pts, inv):
    def kernel(*refs):
        coupling_kernel(mine, *refs)

    return pl.pallas_call(
        kernel,
        out_shape=jax.ShapeDtypeStruct((HALF, PACKED, W), F32),
        in_specs=[HBM, VMEM],
        out_specs=VMEM,
        scratch_shapes=[pltpu.VMEM((HALF, 3, W, W), F32), pltpu.SemaphoreType.DMA((HALF,))],
        cost_estimate=pl.CostEstimate(flops=HALF * 2 * 9 * W * W * W, bytes_accessed=HALF * 4 * W * W * 4, transcendentals=0),
        compiler_params=pltpu.CompilerParams(vmem_limit_bytes=8 << 20),
        name="coupling",
    )(pts, inv)


def prepare_kernel(counts_ref, c0_ref, c1_ref, c2_ref, c3_ref, high_ref, low_ref, t_ref, t_high_ref, t_low_ref):
    live = counts_ref[cluster_device()]
    for k in range(SLOTS // CHUNK):

        @pl.when(k * CHUNK < live)
        def _():
            for slot in range(k * CHUNK, (k + 1) * CHUNK):
                for rel, ref in enumerate((c0_ref, c1_ref, c2_ref, c3_ref)):
                    high, low = split(ref[slot])
                    high_ref[slot, :, rel * W : (rel + 1) * W] = high
                    low_ref[slot, :, rel * W : (rel + 1) * W] = low
                panel_t = c0_ref[slot].T
                t_ref[slot] = panel_t
                t_high_ref[slot], t_low_ref[slot] = split(panel_t)


def in_vmem(values):
    return [pltpu.with_memory_space_constraint(v, pltpu.VMEM) for v in values]


def prepare(counts, panels):
    wide, square = (SLOTS, W, 4 * W), (SLOTS, W, W)
    return pl.pallas_call(
        prepare_kernel,
        out_shape=[
            jax.ShapeDtypeStruct(shape, kind)
            for shape, kind in ((wide, BF16), (wide, BF16), (square, F32), (square, BF16), (square, BF16))
        ],
        in_specs=[SMEM] + [VMEM] * 4,
        out_specs=[VMEM] * 5,
        cost_estimate=pl.CostEstimate(flops=SLOTS * 20 * W * W, bytes_accessed=SLOTS * 12 * W * W * 4, transcendentals=0),
        compiler_params=pltpu.CompilerParams(vmem_limit_bytes=8 << 20),
        name="prepare",
    )(counts, *in_vmem(panels))


def schur_kernel(counts_ref, tiles_ref, own_ref, oth_ref, high_ref, low_ref, t_ref, t_high_ref, t_low_ref, *refs):
    outs, o_sems, accs = refs[:8], refs[8], refs[9:]
    core = lax.axis_index("c")
    cam = camera_index()
    device = cluster_device()
    live = counts_ref[device]
    steps = SLOTS // CHUNK
    for acc in accs:
        acc[...] = jnp.zeros_like(acc)

    for k in range(steps):
        @pl.when(k * CHUNK < live)
        def _():
            for i in range(CHUNK):
                slot = k * CHUNK + i
                packed = jnp.where(core == k // 2, own_ref[slot % HALF], oth_ref[slot % HALF])
                top, rest = packed[: W // 2], packed[W // 2 :]
                corner = jnp.concatenate([rest[:, : W // 2], rest[:, W // 2 :]], axis=0)
                bottom = jnp.concatenate([top[:, W // 2 :].T, corner], axis=1)
                m_high, m_low = split(jnp.concatenate([top, bottom], axis=0))
                t_high, t_low = t_high_ref[slot], t_low_ref[slot]
                prod = jnp.dot(
                    jnp.concatenate([t_high, t_high, t_low], axis=1),
                    jnp.concatenate([m_high, m_low, m_high], axis=0),
                    preferred_element_type=F32,
                )
                rest = t_ref[slot] - prod
                if i:
                    rest = jnp.where(slot < live, rest, 0.0)
                r_high, r_low = split(rest)
                left = jnp.concatenate([r_high, r_high, r_low], axis=1)
                highs = high_ref[slot]
                right = jnp.concatenate([highs, low_ref[slot], highs], axis=0)
                rows = jnp.dot(left, right, preferred_element_type=F32)
                row_tile = tiles_ref[cam, device * SLOTS + slot]
                for rel in range(4):
                    block = rows[:, rel * W : (rel + 1) * W].reshape(NZH, NZL, NYL, 8, W)

                    def add(group, tile, block=block):
                        for zl in range(NZL):
                            for yl in range(NYL):
                                at = {"xl": lax.rem(row_tile, NXL), "zl": zl, "yl": yl}
                                lead = tuple(at[name] for name in GROUPS[group][:3])
                                accs[group][lead + (row_tile // NXL, slice(None), tile)] += block[:, zl, yl]

                    if rel == 0:
                        add(0, GT)
                        continue
                    tile = tiles_ref[lax.bitwise_xor(cam, rel), device * SLOTS + slot]
                    if rel < 3:
                        add(rel - 1, tile)
                        continue
                    last = tile == GT - 1
                    add(1, GT, jnp.where(last, block, 0.0))
                    add(2, jnp.minimum(tile, GT - 2), jnp.where(last, 0.0, block))

    copies = []
    for group, names in enumerate(GROUPS):
        bit = lax.axis_index(names[0])
        away = accs[group].at[1 - bit]
        copies += [away.at[0], away.at[1]] if group < 2 else [away]
        copies.append(accs[group].at[bit])
    copies = [pltpu.make_async_copy(source, outs[k], o_sems.at[k]) for k, source in enumerate(copies)]
    for copy in copies:
        copy.start()
    for copy in copies:
        copy.wait()


def schur(counts, tiles, own, oth, ready):
    return pl.pallas_call(
        schur_kernel,
        out_shape=[
            jax.ShapeDtypeStruct(lead + (2, NXH, NZH, names[3], 8, W), F32) for k, names in enumerate(GROUPS)
            for lead in (((), (), (2,)) if k < 2 else ((2,), (2,)))
        ],
        in_specs=[SMEM, SMEM] + [VMEM] * 7,
        out_specs=[ANY] * 8,
        scratch_shapes=[
            pltpu.SemaphoreType.DMA((8,)),
        ]
        + [pltpu.VMEM((2, 2, 2, NXH, NZH, names[3], 8, W), F32) for names in GROUPS],
        cost_estimate=pl.CostEstimate(flops=SLOTS * 6 * 5 * W * W * W, bytes_accessed=SLOTS * 5 * W * W * 4, transcendentals=0),
        compiler_params=pltpu.CompilerParams(vmem_limit_bytes=12 << 20),
        name="schur",
    )(counts, tiles, *in_vmem((own, oth, *ready)))


def place_kernel(in_ref, out_ref):
    cam = camera_index()
    x = lax.axis_index("xh") * NXL + lax.axis_index("xl")
    out_ref[...] = jnp.zeros_like(out_ref)

    def total(tile):
        value = in_ref[0, tile]
        for source in range(1, NXH * NZH):
            value = value + in_ref[source, tile]
        return value

    row = 0
    for rel, t in [(1, t) for t in range(GT)] + [(0, x)] + [(2, t) for t in range(GT)] + [(3, (t - 1) % GT) for t in range(GT)]:
        column = lax.bitwise_xor(cam, rel) * GT + t
        out_ref[0, :, pl.ds(pl.multiple_of(column * W, W), W)] = total(row)
        row += 1


def place(pieces):
    return pl.pallas_call(
        place_kernel,
        out_shape=jax.ShapeDtypeStruct((1, 8, 4 * GT * W), F32),
        in_specs=[VMEM],
        out_specs=VMEM,
        compiler_params=pltpu.CompilerParams(vmem_limit_bytes=4 << 20),
        name="place",
    )(pieces)


def halve_kernel(axis, keep_ref, *refs):
    parts, send_ref, out_ref = refs[:-2], refs[-2], refs[-1]
    bit = lax.axis_index(axis)
    for at in range(2):
        value = keep_ref[at] + (parts[at][...] if len(parts) == 2 else parts[0][at])

        @pl.when(bit == at)
        def _():
            out_ref[...] = value

        @pl.when(bit != at)
        def _():
            send_ref[...] = value


def halve(axis, keep, parts):
    def kernel(*refs):
        halve_kernel(axis, *refs)

    return pl.pallas_call(
        kernel,
        out_shape=[jax.ShapeDtypeStruct(keep.shape[1:], F32)] * 2,
        in_specs=[VMEM] * (1 + len(parts)),
        out_specs=[VMEM] * 2,
        compiler_params=pltpu.CompilerParams(vmem_limit_bytes=4 << 20),
        name="halve",
    )(*[pltpu.with_memory_space_constraint(v, pltpu.VMEM) for v in (keep, *parts)])


def swap_other(value, high, low, size):
    return lax.ppermute(value, (high, low), [(i, (i + 1 if i % 2 else i - 1) % size) for i in range(size)])


def swap(value, axis):
    return lax.ppermute(value, axis, [(0, 1), (1, 0)])


def on_device(counts, tiles, cam_jac, point_jac, point_inv):
    pts = point_jac.transpose(0, 2, 1, 3)
    inv = point_inv.transpose(1, 2, 0, 3)

    c0 = cam_jac
    c2 = swap(c0, "yh")
    c1 = swap(c0, "c")
    m_send = coupling(False, pts, inv)
    m_recv = swap(m_send, "c")
    m_keep = coupling(True, pts, inv)
    m_chip = m_keep + m_recv
    m_recv = swap(m_chip, "yh")
    c3 = swap(c2, "c")
    ready = prepare(counts, (c0, c1, c2, c3))
    m_own = m_chip + m_recv
    m_oth = swap(m_own, "c")
    outs = schur(counts, tiles.T, m_own, m_oth, ready)
    near_y = swap(outs[6], "yl")
    low_z = swap(outs[3], "zl")
    low_x = swap(outs[0], "xl")
    high_z = swap_other(outs[4], "zh", "zl", NZH * NZL)
    high_x = swap_other(outs[1], "xh", "xl", NXH * NXL)
    groups = [(outs[2], (low_x, high_x)), (outs[5], (low_z, high_z)), (outs[7], (near_y,))]
    for phase in (1, 2):
        halves = []
        for k, (keep, parts) in enumerate(groups):
            halves.append(halve(GROUPS[k][phase], keep, parts))
        groups = []
        for k, (send, keep) in enumerate(halves):
            groups.append((keep, (swap(send, GROUPS[k][phase]),)))
    groups = [(keep, parts[0]) for keep, parts in groups]
    received = [got for _, got in groups]
    part = jnp.concatenate(
        [(keep + got).reshape(NXH * NZH, -1, 8, W) for (keep, _), got in zip(groups, received)], axis=1
    )
    return place(lax.all_to_all(part, ("xh", "zh"), 0, 0, tiled=True))


def solution(mesh):
    fine = Mesh(mesh.devices.reshape(NXH, NXL, NZH, NZL, NYL, 2, 2), ("xh", "xl", "zh", "zl", "yl", "yh", "c"))
    rows = ("xh", "xl", "zh", "zl", "yl")
    cams = ("yh", "c")
    in_specs = (
        P(),
        P(),
        P(rows, None, cams),
        P(rows, None, None, cams),
        P(rows, None, None, cams),
    )
    return jax.shard_map(
        on_device, mesh=fine, in_specs=in_specs, out_specs=P(cams, rows, None), check_vma=False
    )
```

```python
import jax
import jax.numpy as jnp
from jax import lax
from jax.experimental import pallas as pl
from jax.experimental.pallas import tpu as pltpu
from jax.sharding import Mesh, PartitionSpec as P


W = 128
SLOTS = 16
HALF = SLOTS // 2
CHUNK = 4
PACKED = 3 * W // 4
GT = 4
NXH, NXL, NZH, NZL, NYL = 2, 2, 4, 2, 2
GROUPS = (("xl", "zl", "yl", GT + 1), ("zl", "yl", "xl", GT), ("yl", "xl", "zl", GT))
F32 = jnp.float32
BF16 = jnp.bfloat16
ANY = pl.BlockSpec(memory_space=pl.ANY)
SMEM = pl.BlockSpec(memory_space=pltpu.SMEM)
VMEM = pl.BlockSpec(memory_space=pltpu.VMEM)
HBM = pl.BlockSpec(memory_space=pltpu.HBM)


def split(value):
    high = value.astype(BF16)
    return high, (value - high.astype(F32)).astype(BF16)


def camera_index():
    return lax.axis_index("yh") * 2 + lax.axis_index("c")


def cluster_device():
    xh, xl, zh, zl, yl = (lax.axis_index(name) for name in ("xh", "xl", "zh", "zl", "yl"))
    return (((xh * NXL + xl) * NZH + zh) * NZL + zl) * NYL + yl


def coupling_kernel(mine, pts_hbm, inv_ref, out_ref, pts_buf, sems):
    core = lax.axis_index("c")
    base = (core if mine else 1 - core) * HALF

    def fetch(i):
        return pltpu.make_async_copy(pts_hbm.at[base + i], pts_buf.at[i], sems.at[i])

    for i in range(HALF):
        fetch(i).start()
    for i in range(HALF):
        fetch(i).wait()
        pts = [pts_buf[i, j] for j in range(3)]
        pairs = []
        for k in range(3):
            weighted = None
            for j in range(3):
                term = pts[j] * inv_ref[j, k, pl.ds(base + i, 1), :]
                weighted = term if weighted is None else weighted + term
            pairs.append((split(weighted), split(pts[k])))
        left = jnp.concatenate([w[0] for w, _ in pairs] + [w[0] for w, _ in pairs] + [w[1] for w, _ in pairs], axis=1)
        right = jnp.concatenate([p[0] for _, p in pairs] + [p[1] for _, p in pairs] + [p[0] for _, p in pairs], axis=1)
        full = lax.dot_general(left, right, (((1,), (1,)), ((), ())), preferred_element_type=F32)
        out_ref[i, : W // 2] = full[: W // 2]
        out_ref[i, W // 2 :, : W // 2] = full[W // 2 : PACKED, W // 2 :]
        out_ref[i, W // 2 :, W // 2 :] = full[PACKED:, W // 2 :]


def coupling(mine, pts, inv):
    def kernel(*refs):
        coupling_kernel(mine, *refs)

    return pl.pallas_call(
        kernel,
        out_shape=jax.ShapeDtypeStruct((HALF, PACKED, W), F32),
        in_specs=[HBM, VMEM],
        out_specs=VMEM,
        scratch_shapes=[pltpu.VMEM((HALF, 3, W, W), F32), pltpu.SemaphoreType.DMA((HALF,))],
        cost_estimate=pl.CostEstimate(flops=HALF * 2 * 9 * W * W * W, bytes_accessed=HALF * 4 * W * W * 4, transcendentals=0),
        compiler_params=pltpu.CompilerParams(vmem_limit_bytes=8 << 20),
        name="coupling",
    )(pts, inv)


def prepare_kernel(counts_ref, c0_ref, c1_ref, c2_ref, c3_ref, high_ref, low_ref, t_ref, t_high_ref, t_low_ref):
    live = counts_ref[cluster_device()]
    for k in range(SLOTS // CHUNK):

        @pl.when(k * CHUNK < live)
        def _():
            for slot in range(k * CHUNK, (k + 1) * CHUNK):
                for rel, ref in enumerate((c0_ref, c1_ref, c2_ref, c3_ref)):
                    high, low = split(ref[slot])
                    high_ref[slot, :, rel * W : (rel + 1) * W] = high
                    low_ref[slot, :, rel * W : (rel + 1) * W] = low
                panel_t = c0_ref[slot].T
                t_ref[slot] = panel_t
                t_high_ref[slot], t_low_ref[slot] = split(panel_t)


def in_vmem(values):
    return [pltpu.with_memory_space_constraint(v, pltpu.VMEM) for v in values]


def prepare(counts, panels):
    wide, square = (SLOTS, W, 4 * W), (SLOTS, W, W)
    return pl.pallas_call(
        prepare_kernel,
        out_shape=[
            jax.ShapeDtypeStruct(shape, kind)
            for shape, kind in ((wide, BF16), (wide, BF16), (square, F32), (square, BF16), (square, BF16))
        ],
        in_specs=[SMEM] + [VMEM] * 4,
        out_specs=[VMEM] * 5,
        cost_estimate=pl.CostEstimate(flops=SLOTS * 20 * W * W, bytes_accessed=SLOTS * 12 * W * W * 4, transcendentals=0),
        compiler_params=pltpu.CompilerParams(vmem_limit_bytes=8 << 20),
        name="prepare",
    )(counts, *in_vmem(panels))


def schur_kernel(counts_ref, tiles_ref, own_ref, oth_ref, high_ref, low_ref, t_ref, t_high_ref, t_low_ref, *refs):
    outs, o_sems, accs = refs[:7], refs[7], refs[8:]
    core = lax.axis_index("c")
    cam = camera_index()
    device = cluster_device()
    live = counts_ref[device]
    steps = SLOTS // CHUNK
    for acc in accs:
        acc[...] = jnp.zeros_like(acc)

    for k in range(steps):
        @pl.when(k * CHUNK < live)
        def _():
            for i in range(CHUNK):
                slot = k * CHUNK + i
                packed = jnp.where(core == k // 2, own_ref[slot % HALF], oth_ref[slot % HALF])
                top, rest = packed[: W // 2], packed[W // 2 :]
                corner = jnp.concatenate([rest[:, : W // 2], rest[:, W // 2 :]], axis=0)
                bottom = jnp.concatenate([top[:, W // 2 :].T, corner], axis=1)
                m_high, m_low = split(jnp.concatenate([top, bottom], axis=0))
                t_high, t_low = t_high_ref[slot], t_low_ref[slot]
                prod = jnp.dot(
                    jnp.concatenate([t_high, t_high, t_low], axis=1),
                    jnp.concatenate([m_high, m_low, m_high], axis=0),
                    preferred_element_type=F32,
                )
                rest = t_ref[slot] - prod
                if i:
                    rest = jnp.where(slot < live, rest, 0.0)
                r_high, r_low = split(rest)
                left = jnp.concatenate([r_high, r_high, r_low], axis=1)
                highs = high_ref[slot]
                right = jnp.concatenate([highs, low_ref[slot], highs], axis=0)
                rows = jnp.dot(left, right, preferred_element_type=F32)
                row_tile = tiles_ref[cam, device * SLOTS + slot]
                for rel in range(4):
                    block = rows[:, rel * W : (rel + 1) * W].reshape(NZH, NZL, NYL, 8, W)

                    def add(group, tile, block=block):
                        for zl in range(NZL):
                            for yl in range(NYL):
                                at = {"xl": lax.rem(row_tile, NXL), "zl": zl, "yl": yl}
                                lead = tuple(at[name] for name in GROUPS[group][:3])
                                accs[group][lead + (row_tile // NXL, slice(None), tile)] += block[:, zl, yl]

                    if rel == 0:
                        add(0, GT)
                        continue
                    tile = tiles_ref[lax.bitwise_xor(cam, rel), device * SLOTS + slot]
                    add(rel - 1, tile)

    copies = []
    for group, names in enumerate(GROUPS):
        bit = lax.axis_index(names[0])
        away = accs[group].at[1 - bit]
        copies += [away.at[0], away.at[1]] if group == 0 else [away]
        copies.append(accs[group].at[bit])
    copies = [pltpu.make_async_copy(source, outs[k], o_sems.at[k]) for k, source in enumerate(copies)]
    for copy in copies:
        copy.start()
    for copy in copies:
        copy.wait()


def schur(counts, tiles, own, oth, ready):
    return pl.pallas_call(
        schur_kernel,
        out_shape=[
            jax.ShapeDtypeStruct(lead + (2, NXH, NZH, names[3], 8, W), F32) for k, names in enumerate(GROUPS)
            for lead in (((), (), (2,)) if k == 0 else ((2,), (2,)))
        ],
        in_specs=[SMEM, SMEM] + [VMEM] * 7,
        out_specs=[ANY] * 7,
        scratch_shapes=[
            pltpu.SemaphoreType.DMA((7,)),
        ]
        + [pltpu.VMEM((2, 2, 2, NXH, NZH, names[3], 8, W), F32) for names in GROUPS],
        cost_estimate=pl.CostEstimate(flops=SLOTS * 6 * 5 * W * W * W, bytes_accessed=SLOTS * 5 * W * W * 4, transcendentals=0),
        compiler_params=pltpu.CompilerParams(vmem_limit_bytes=12 << 20),
        name="schur",
    )(counts, tiles, *in_vmem((own, oth, *ready)))


def place_kernel(in_ref, out_ref):
    cam = camera_index()
    x = lax.axis_index("xh") * NXL + lax.axis_index("xl")
    out_ref[...] = jnp.zeros_like(out_ref)

    def total(tile):
        value = in_ref[0, tile]
        for source in range(1, NXH * NZH):
            value = value + in_ref[source, tile]
        return value

    row = 0
    for rel, t in [(1, t) for t in range(GT)] + [(0, x)] + [(rel, t) for rel in (2, 3) for t in range(GT)]:
        column = lax.bitwise_xor(cam, rel) * GT + t
        out_ref[0, :, pl.ds(pl.multiple_of(column * W, W), W)] = total(row)
        row += 1


def place(pieces):
    return pl.pallas_call(
        place_kernel,
        out_shape=jax.ShapeDtypeStruct((1, 8, 4 * GT * W), F32),
        in_specs=[VMEM],
        out_specs=VMEM,
        compiler_params=pltpu.CompilerParams(vmem_limit_bytes=4 << 20),
        name="place",
    )(pieces)


def halve_kernel(axis, keep_ref, *refs):
    parts, send_ref, out_ref = refs[:-2], refs[-2], refs[-1]
    bit = lax.axis_index(axis)
    for at in range(2):
        value = keep_ref[at] + (parts[at][...] if len(parts) == 2 else parts[0][at])

        @pl.when(bit == at)
        def _():
            out_ref[...] = value

        @pl.when(bit != at)
        def _():
            send_ref[...] = value


def halve(axis, keep, parts):
    def kernel(*refs):
        halve_kernel(axis, *refs)

    return pl.pallas_call(
        kernel,
        out_shape=[jax.ShapeDtypeStruct(keep.shape[1:], F32)] * 2,
        in_specs=[VMEM] * (1 + len(parts)),
        out_specs=[VMEM] * 2,
        compiler_params=pltpu.CompilerParams(vmem_limit_bytes=4 << 20),
        name="halve",
    )(*[pltpu.with_memory_space_constraint(v, pltpu.VMEM) for v in (keep, *parts)])


def swap_x_other(value):
    size = NXH * NXL
    return lax.ppermute(value, ("xh", "xl"), [(i, (i + 1 if i % 2 else i - 1) % size) for i in range(size)])


def swap(value, axis):
    return lax.ppermute(value, axis, [(0, 1), (1, 0)])


def on_device(counts, tiles, cam_jac, point_jac, point_inv):
    pts = point_jac.transpose(0, 2, 1, 3)
    inv = point_inv.transpose(1, 2, 0, 3)

    c0 = cam_jac
    c2 = swap(c0, "yh")
    c1 = swap(c0, "c")
    m_send = coupling(False, pts, inv)
    m_recv = swap(m_send, "c")
    m_keep = coupling(True, pts, inv)
    m_chip = m_keep + m_recv
    m_recv = swap(m_chip, "yh")
    c3 = swap(c2, "c")
    ready = prepare(counts, (c0, c1, c2, c3))
    m_own = m_chip + m_recv
    m_oth = swap(m_own, "c")
    outs = schur(counts, tiles.T, m_own, m_oth, ready)
    near_z = swap(outs[3], "zl")
    near_y = swap(outs[5], "yl")
    low_x = swap(outs[0], "xl")
    high_x = swap_x_other(outs[1])
    groups = [(outs[2], (low_x, high_x)), (outs[4], (near_z,)), (outs[6], (near_y,))]
    for phase in (1, 2):
        halves = []
        for k, (keep, parts) in enumerate(groups):
            halves.append(halve(GROUPS[k][phase], keep, parts))
        groups = []
        for k, (send, keep) in enumerate(halves):
            groups.append((keep, (swap(send, GROUPS[k][phase]),)))
    groups = [(keep, parts[0]) for keep, parts in groups]
    received = [got for _, got in groups]
    part = jnp.concatenate(
        [(keep + got).reshape(NXH * NZH, -1, 8, W) for (keep, _), got in zip(groups, received)], axis=1
    )
    return place(lax.all_to_all(part, ("xh", "zh"), 0, 0, tiled=True))


def solution(mesh):
    fine = Mesh(mesh.devices.reshape(NXH, NXL, NZH, NZL, NYL, 2, 2), ("xh", "xl", "zh", "zl", "yl", "yh", "c"))
    rows = ("xh", "xl", "zh", "zl", "yl")
    cams = ("yh", "c")
    in_specs = (
        P(),
        P(),
        P(rows, None, cams),
        P(rows, None, None, cams),
        P(rows, None, None, cams),
    )
    return jax.shard_map(
        on_device, mesh=fine, in_specs=in_specs, out_specs=P(cams, rows, None), check_vma=False
    )
```
